128 devices in a mesh: ctx: 16 (over y, x), head: 8 (over z, core).
Axes of the slice: x: 4, y: 4, z: 4, core: 2. Of those that a mesh axis runs over, the one named last changes fastest.
Arguments:
- branch_rows: bfloat16 [16384, 2048], P(('ctx', 'head')), may hold values from -6 to 6
- expert_ids: int32 [16384, 8], P(('ctx', 'head')), may hold values from 0 to 127, all different within a row; in each aligned block of 128 rows (0 to 127, 128 to 255, ...) at most 12 rows name the same one
- targets: int32 [16384], P(('ctx', 'head')), may hold values from 0 to 8191, as said below
- router: bfloat16 [2048, 128], replicated, may hold values from -0.046875 to 0.046875
- w_gate: bfloat16 [128, 2048, 768], P(('ctx', 'head')), may hold values from -0.125 to 0.125
- w_up: bfloat16 [128, 2048, 768], P(('ctx', 'head')), may hold values from -0.125 to 0.125
- w_down: bfloat16 [128, 768, 2048], P(('ctx', 'head')), may hold values from -0.3125 to 0.3125
- stream: bfloat16 [8192, 2048], P('ctx', 'head'), may hold values from -6 to 6
- attn_gain: float32 [2048], replicated, may hold values from 0.1 to 1.9
- q_gain: float32 [4096], P('head'), may hold values from 0.5 to 7
- k_gain: float32 [512], replicated, may hold values from 0.8 to 6
- w_query: bfloat16 [2048, 4096], P(None, 'head')
- w_key: bfloat16 [2048, 512], replicated
- w_value: bfloat16 [2048, 512], replicated, may hold values from -0.125 to 0.125
- w_out: bfloat16 [4096, 2048], P('head'), may hold values from -0.375 to 0.375
Outputs:
- layer_out: bfloat16 [8192, 2048], P('ctx', 'head')
The draws below stay inside these ranges and needn't reach their ends.
Inputs may be any that keep to these rules, and one draw needn't show every extreme that they name: `expert_ids`: in each device's 128 rows no expert is named more than 12 times. `targets`: each device's 128 rows name exactly 8 positions in each block of 512 joined positions; positions may repeat.
All inputs are finite; a program needn't handle non-finite values.
Results may differ from the reference program's by a relative error of at most 0.018.
Values may be sent and summed in bfloat16 or wider, within the bound.
No kernel may reach another device: no remote copies, remote signals or barrier semaphores. Data moves between devices by JAX's collectives and lax.ppermute only.
A program may use at most 192 MiB of HBM per device.

```python
import math
import jax
import jax.numpy as jnp
import numpy as np
from jax import lax

D = 2048
FF = 768
TOP = 8
QH = 32
KVH = 4
HD = 128
ROWS_DEV = 128
TOKC = 512
EXPERTS = 128
ROWS = 16384
SEQ = 8192
CAP = 12
RPO = 8
N_CTX = 16
N_HEAD = 8


def draw_targets(key, part):
    blocks = ROWS // ROWS_DEV
    owners = SEQ // TOKC
    spots = jax.random.randint(jax.random.fold_in(key, 11), (blocks, owners, RPO), 0, TOKC, dtype=jnp.int32)
    offsets = (jnp.arange(owners, dtype=jnp.int32) * TOKC)[None, :, None]
    placed = (spots + offsets).reshape(blocks, ROWS_DEV)
    block_keys = jax.random.split(jax.random.fold_in(key, 12), blocks)
    orders = jax.vmap(lambda block_key: jax.random.permutation(block_key, ROWS_DEV))(block_keys)
    return jnp.take_along_axis(placed, orders, 1).reshape(ROWS).astype(jnp.int32)


def query_key_pair(key):
    query_part = jax.random.truncated_normal(jax.random.fold_in(key, 21), -6.0, 6.0, (D, QH * HD), jnp.float32) / math.sqrt(D)
    key_part = jax.random.truncated_normal(jax.random.fold_in(key, 22), -6.0, 6.0, (D, KVH * HD), jnp.float32) / math.sqrt(D)
    return (query_part, key_part)


def draw_w_query(key, part):
    return query_key_pair(key)[0].astype(jnp.bfloat16)


def draw_w_key(key, part):
    return query_key_pair(key)[1].astype(jnp.bfloat16)


def draw_q_gain(key, part):
    return jnp.exp(jax.random.uniform(jax.random.fold_in(key, 33), (QH * HD,), jnp.float32, math.log(0.8), math.log(2.0)))


def draw_k_gain(key, part):
    return jnp.exp(jax.random.uniform(jax.random.fold_in(key, 42), (KVH * HD,), jnp.float32, math.log(0.8), math.log(2.0)))


def block_scale(rng, shape, pieces, low, largest):
    gain, own = 1.0, jax.random.fold_in(rng, 6)
    for position, shards_of in pieces:
        heights = jnp.exp(jax.random.uniform(jax.random.fold_in(own, position), (shards_of,), jnp.float32, low / len(pieces), largest / len(pieces)))
        gain = gain * jnp.repeat(heights, shape[position] // shards_of).reshape([-1 if axis == position else 1 for axis in range(len(shape))])
    return gain


def shared_out(rng, own, number, rows, number_of, top, reach, slope):
    sequence = jax.random.permutation(rng, number_of)
    packed, usual = portions_of(number_of, rows * top, reach, slope, True), portions_of(number_of, rows * top, reach, slope, False)
    places = jnp.arange(number_of)

    def named(tallies, offset_by):
        used = int((tallies > 0).sum())
        fixed = max(1, used // 4)
        passed = fixed + (places - fixed + offset_by * (used - fixed)) % max(1, number_of - fixed)
        return jnp.zeros((number_of,), jnp.int32).at[sequence[jnp.where(places < fixed, places, passed)]].set(jnp.asarray(tallies, jnp.int32))

    tallies = jnp.where(number % 4 == 0, named(packed, number // 4), named(usual, number - number // 4 - 1))
    mixed = jax.random.permutation(jax.random.fold_in(own, 3), number_of)
    donor, sink = mixed[0:number_of // 2 * 2:2], mixed[1:number_of // 2 * 2:2]
    slack = jnp.minimum(tallies[donor] - 1, reach - tallies[sink]) // 2
    slack = jnp.where((donor == sequence[0]) | (sink == sequence[0]) | (tallies[sink] == 0), 0, jnp.maximum(slack, 0))
    passed = jax.random.randint(jax.random.fold_in(own, 4), (number_of // 2,), 0, 1 << 20) % (slack + 1)
    tallies = tallies.at[donor].add(-passed).at[sink].add(passed)
    members = jnp.searchsorted(jnp.cumsum(tallies), jnp.arange(rows * top), side="right").astype(jnp.int32)
    listing = members.reshape(top, rows).T
    listing = listing[jax.random.permutation(jax.random.fold_in(own, 1), rows)]
    offset_by = jax.random.randint(jax.random.fold_in(own, 2), (rows, 1), 0, top)
    return jnp.take_along_axis(listing, (jnp.arange(top)[None, :] + offset_by) % top, axis=1)


def portions_of(number_of, total, most, slope, full):
    weights = [(1 << 20) // math.isqrt(standing ** slope) + 1 for standing in range(1, number_of + 1)]
    largest = most if full else min(most, max(-(-total // number_of), total * weights[0] // sum(weights)))
    least = 1 if total - largest >= number_of - 1 else 0
    holding, rest = [largest] + [least] * (number_of - 1), total - largest - least * (number_of - 1)
    while rest > 0:
        candidates = [i for i in range(1, number_of) if holding[i] < largest] or [i for i in range(1, number_of) if holding[i] < most]
        mass, remaining = sum([weights[i] for i in candidates]), rest
        for i in candidates:
            more = min(most - holding[i], max(1, remaining * weights[i] // mass), rest)
            holding[i] = holding[i] + more
            rest = rest - more
    return np.array(holding)


def normal_values(stream_key, dims, spread, most, cuts=(), kind=jnp.bfloat16):
    entries = spread * jax.random.normal(stream_key, dims, jnp.float32)
    if cuts:
        entries = entries * block_scale(stream_key, dims, cuts, -0.22, 0.18)
    return jnp.clip(entries, -most, most).astype(kind)


def setup_inputs(seed: int = 0) -> dict:
    arg_keys = jax.random.split(jax.random.key(seed), 16)
    branch_rows = normal_values(arg_keys[0], (ROWS, D), 1.0, 6.0, ((0, 128),))
    expert_ids_keys = jax.random.split(jax.random.fold_in(arg_keys[1], 1), ROWS // ROWS_DEV)
    expert_ids_turns = jax.random.permutation(jax.random.fold_in(arg_keys[1], 3), ROWS // ROWS_DEV)
    expert_ids = jax.vmap(lambda own, number: shared_out(jax.random.fold_in(arg_keys[1], 2), own, number, ROWS_DEV, EXPERTS, TOP, CAP, 2))(expert_ids_keys, expert_ids_turns).reshape((ROWS, TOP))
    targets = draw_targets(jax.random.fold_in(arg_keys[15], 71), 0)
    router = normal_values(arg_keys[3], (D, EXPERTS), (8 * D) ** -0.5, 0.046875)
    w_gate = normal_values(arg_keys[4], (EXPERTS, D, FF), D ** -0.5, 0.125, ((0, 128),))
    w_up = normal_values(arg_keys[5], (EXPERTS, D, FF), D ** -0.5, 0.125, ((0, 128),))
    w_down = normal_values(arg_keys[6], (EXPERTS, FF, D), (FF // 2) ** -0.5, 0.3125, ((0, 128),))
    stream = normal_values(arg_keys[7], (SEQ, D), 1.0, 6.0, ((0, 16), (1, 8)))
    attn_gain = jnp.clip(1.0 + 0.18 * jax.random.normal(arg_keys[8], (D,), jnp.float32), 0.1, 1.9)
    q_gain = draw_q_gain(jax.random.fold_in(arg_keys[15], 71), 0)
    k_gain = draw_k_gain(jax.random.fold_in(arg_keys[15], 71), 0)
    w_query = draw_w_query(jax.random.fold_in(arg_keys[15], 71), 0)
    w_key = draw_w_key(jax.random.fold_in(arg_keys[15], 71), 0)
    w_value = normal_values(arg_keys[13], (D, KVH * HD), D ** -0.5, 0.125)
    w_out = normal_values(arg_keys[14], (QH * HD, D), (2 * HD) ** -0.5, 0.375, ((0, 8),))
    return dict(branch_rows=branch_rows, expert_ids=expert_ids, targets=targets, router=router, w_gate=w_gate, w_up=w_up, w_down=w_down, stream=stream, attn_gain=attn_gain, q_gain=q_gain, k_gain=k_gain, w_query=w_query, w_key=w_key, w_value=w_value, w_out=w_out)


EPSILON = 1e-06
THETA = 1000000.0

def rotary(vectors, positions):
    half_dim = vectors.shape[-1] // 2
    frequency = jnp.power(jnp.float32(THETA), -jnp.arange(half_dim, dtype=jnp.float32) * 2.0 / vectors.shape[-1])
    angles = positions.astype(jnp.float32)[:, None] * frequency[None, :]
    cosines = jnp.cos(angles)[:, None, :]
    sines = jnp.sin(angles)[:, None, :]
    front_part = vectors[..., :half_dim]
    back_part = vectors[..., half_dim:]
    return jnp.concatenate([front_part * cosines - back_part * sines, back_part * cosines + front_part * sines], -1)

def head_norm(vectors, scales):
    return vectors * lax.rsqrt(lax.optimization_barrier(jnp.mean(vectors * vectors, -1, keepdims=True)) + EPSILON) * scales

def expert_rows(inputs, gate_proj, up_proj, down_proj):
    gate_part = jnp.dot(inputs, gate_proj, preferred_element_type=jnp.float32)
    upward = jnp.dot(inputs, up_proj, preferred_element_type=jnp.float32)
    hidden = (jax.nn.silu(gate_part) * upward).astype(jnp.bfloat16)
    return jnp.dot(hidden, down_proj, preferred_element_type=jnp.float32).astype(jnp.bfloat16)

def slot_index(expert_block):
    flat_ids = expert_block.reshape(-1)
    onehot = (flat_ids[:, None] == jnp.arange(EXPERTS, dtype=jnp.int32)[None, :]).astype(jnp.int32)
    earlier = jnp.cumsum(onehot, 0) - onehot
    return lax.optimization_barrier(jnp.sum(earlier * onehot, 1)).astype(jnp.int32)

def reference(branch_rows, expert_ids, targets, router, w_gate, w_up, w_down, stream, attn_gain, q_gain, k_gain, w_query, w_key, w_value, w_out):
    devices = N_CTX * N_HEAD
    logits = jnp.dot(branch_rows, router, preferred_element_type=jnp.float32)
    chosen = expert_ids[:, :, None] == jnp.arange(EXPERTS, dtype=jnp.int32)[None, None, :]
    picked = lax.optimization_barrier(jnp.sum(jnp.where(chosen, logits[:, None, :], 0.0), -1))
    gate_probs = jax.nn.softmax(picked, -1)
    blocks = expert_ids.reshape(devices, ROWS_DEV, TOP)
    slots = jax.vmap(slot_index)(blocks)
    expert_flat = blocks.reshape(devices, ROWS_DEV * TOP)
    columns = (jnp.arange(devices, dtype=jnp.int32)[:, None] * CAP + slots).astype(jnp.int32)
    repeated = jnp.repeat(branch_rows, TOP, axis=0).reshape(devices, ROWS_DEV * TOP, D)
    buffer = jnp.zeros((EXPERTS, devices * CAP, D), jnp.bfloat16).at[expert_flat, columns].set(repeated)
    expert_out = lax.map(lambda operands: expert_rows(operands[0], operands[1], operands[2], operands[3]), (buffer, w_gate, w_up, w_down))
    gathered_out = expert_out[expert_flat, columns].reshape(ROWS, TOP, D)
    merged = jnp.zeros((ROWS, D), jnp.float32)
    for which in range(TOP):
        merged = merged + gate_probs[:, which, None] * gathered_out[:, which].astype(jnp.float32)
    merged = merged.astype(jnp.bfloat16)
    joined = stream.astype(jnp.float32).at[targets].add(merged.astype(jnp.float32)).astype(jnp.bfloat16)
    joined_f = joined.astype(jnp.float32)
    normed = (joined_f * lax.rsqrt(lax.optimization_barrier(jnp.mean(joined_f * joined_f, -1, keepdims=True)) + EPSILON) * attn_gain).astype(jnp.bfloat16)
    positions = jnp.arange(SEQ, dtype=jnp.int32)
    queries = jnp.dot(normed, w_query, preferred_element_type=jnp.float32).reshape(SEQ, QH, HD)
    queries = rotary(head_norm(queries, q_gain.reshape(QH, HD)), positions).astype(jnp.bfloat16)
    key_rows = jnp.dot(normed, w_key, preferred_element_type=jnp.float32).reshape(SEQ, KVH, HD)
    key_rows = rotary(head_norm(key_rows, k_gain.reshape(KVH, HD)), positions).astype(jnp.bfloat16)
    values = jnp.dot(normed, w_value, preferred_element_type=jnp.float32).astype(jnp.bfloat16).reshape(SEQ, KVH, HD)
    group_size = QH // KVH
    head_queries = queries.transpose(1, 0, 2)
    head_keys = jnp.repeat(key_rows.transpose(1, 0, 2), group_size, axis=0)
    head_values = jnp.repeat(values.transpose(1, 0, 2), group_size, axis=0)
    causal = positions[:, None] >= positions[None, :]

    def one_head(operands):
        scores = jnp.dot(operands[0], operands[1].T, preferred_element_type=jnp.float32) / math.sqrt(HD)
        highest = lax.optimization_barrier(jnp.max(jnp.where(causal, scores, -1e+30), -1))
        weights = jnp.where(causal, jnp.exp(scores - highest[:, None]), 0.0)
        totals = lax.optimization_barrier(jnp.sum(weights, -1))
        summed = jnp.dot(weights.astype(jnp.bfloat16), operands[2], preferred_element_type=jnp.float32)
        return (summed / totals[:, None]).astype(jnp.bfloat16)
    attended = lax.map(one_head, (head_queries, head_keys, head_values))
    attended = attended.transpose(1, 0, 2).reshape(SEQ, QH * HD)
    group_cols = QH * HD // N_HEAD
    projected = jnp.zeros((SEQ, D), jnp.float32)
    for group in range(N_HEAD):
        part_out = jnp.dot(attended[:, group * group_cols:(group + 1) * group_cols], w_out[group * group_cols:(group + 1) * group_cols], preferred_element_type=jnp.float32)
        rounded = lax.optimization_barrier(part_out.astype(jnp.bfloat16))
        projected = projected + rounded.astype(jnp.float32)
    layer_out = (joined_f + projected).astype(jnp.bfloat16)
    return layer_out
```

```python
import math

import jax
import jax.numpy as jnp
from jax import lax
from jax.experimental import pallas as pl
from jax.experimental.pallas import tpu as pltpu
from jax.sharding import PartitionSpec as P

QH = 32
KVH = 4
HD = 128
EPSILON = 1e-06
THETA = 1000000.0
F32 = jnp.float32
BF16 = jnp.bfloat16
VMEM = pltpu.VMEM
NEG = -1e30


def iota(shape, dim):
    return lax.broadcasted_iota(jnp.int32, shape, dim)


def dot(a, b):
    return jnp.dot(a, b, preferred_element_type=F32)


def dot_t(a, b):
    return lax.dot_general(a, b, (((1,), (1,)), ((), ())), preferred_element_type=F32)


def dispatch_kernel(rows_ref, ids_ref, trow_ref, tcol_ref, router_ref, y_ref, rank_ref, gate_ref, spot_ref, rows_s, rank_s):
    step = pl.program_id(0)
    experts = 128
    blk = y_ref.shape[0] // 8

    @pl.when(step == 0)
    def _():
        n = rows_ref.shape[0]
        first = iota((n, n), 0)
        second = iota((n, n), 1)
        owner_row = trow_ref[...] // 512
        owner_col = tcol_ref[...] // 512
        same = jnp.where((owner_col == owner_row) & (first < second), 1.0, 0.0)
        place = owner_row.astype(F32) * 8.0 + jnp.sum(same, 0, keepdims=True)
        perm = jnp.where(first.astype(F32) == place, 1.0, 0.0)
        spot = (trow_ref[...] % 512).astype(F32)
        spot_ref[...] = jnp.broadcast_to(jnp.sum(perm * spot, 1, keepdims=True), (n, 128))
        perm_b = perm.astype(BF16)
        rows = dot(perm_b, rows_ref[...]).astype(BF16)
        rows_s[...] = rows
        ids = dot_t(ids_ref[...].astype(F32).astype(BF16), perm_b)
        expert = iota((experts, n), 0).astype(F32)
        member = jnp.zeros((experts, n), F32)
        for k in range(ids.shape[0]):
            member = member + jnp.where(expert == ids[k : k + 1, :], 1.0, 0.0)
        before = jnp.where(first < second, 1.0, 0.0).astype(BF16)
        rank = jnp.where(member > 0.5, dot(member.astype(BF16), before), -1.0)
        rank_s[...] = rank.astype(BF16)
        rank_ref[...] = rank.T
        member_q = member.T > 0.5
        logits = dot(rows, router_ref[...])
        highest = jnp.max(jnp.where(member_q, logits, NEG), 1, keepdims=True)
        raised = jnp.where(member_q, jnp.exp(jnp.minimum(logits - highest, 0.0)), 0.0)
        gate_ref[...] = raised / jnp.sum(raised, 1, keepdims=True)

    spread = jnp.where(iota((blk * 8, experts), 0) // 8 + step * blk == iota((blk * 8, experts), 1), 1.0, 0.0).astype(BF16)
    rank_e = dot(spread, rank_s[...])
    slot = (iota(rank_e.shape, 0) % 8).astype(F32)
    main = jnp.where(rank_e == slot, 1.0, 0.0).astype(BF16)
    low = jnp.where((rank_e == slot + 8.0) & (slot < 4.0), 1.0, 0.0).astype(BF16)
    high = jnp.where((rank_e == slot + 4.0) & (slot >= 4.0), 1.0, 0.0).astype(BF16)
    half = rows_s.shape[1] // 2
    y_ref[:, : 2 * half] = dot(main, rows_s[...]).astype(BF16)
    y_ref[:, 2 * half :] = (dot(low, rows_s[:, :half]) + dot(high, rows_s[:, half:])).astype(BF16)


def dispatch(rows, ids, targets, router):
    n, width = rows.shape
    steps = 4
    whole = lambda shape: pl.BlockSpec(shape, lambda i: tuple(0 for _ in shape))
    return pl.pallas_call(
        dispatch_kernel,
        grid=(steps,),
        in_specs=[whole((n, width)), whole((8, n)), whole((1, n)), whole((n, 1)), whole(router.shape)],
        out_specs=[
            pl.BlockSpec((1024 // steps, width * 3 // 2), lambda i: (i, 0)),
            whole((n, 128)),
            whole((n, 128)),
            whole((n, 128)),
        ],
        out_shape=[
            jax.ShapeDtypeStruct((1024, width * 3 // 2), BF16),
            jax.ShapeDtypeStruct((n, 128), F32),
            jax.ShapeDtypeStruct((n, 128), F32),
            jax.ShapeDtypeStruct((n, 128), F32),
        ],
        scratch_shapes=[VMEM((n, width), BF16), VMEM((128, n), BF16)],
        compiler_params=pltpu.CompilerParams(vmem_limit_bytes=40 * 1024 * 1024),
        name="dispatch_rows",
    )(rows, ids.T, targets.reshape(1, n), targets.reshape(n, 1), router)


def expert_kernel(y_ref, wg_ref, wu_ref, wd_ref, o_ref):
    rows = y_ref.shape[0]
    half_rows = rows // 2
    width = wg_ref.shape[0]
    half = width // 2
    r = iota((half_rows, rows), 0)
    col = iota((half_rows, rows), 1)
    source = r // 4 * 8 + r % 4
    low = jnp.where(col == source, 1.0, 0.0).astype(BF16)
    high = jnp.where(col == source + 4, 1.0, 0.0).astype(BF16)
    extra = y_ref[:, width:]
    inputs = jnp.concatenate(
        [
            y_ref[:, :width],
            jnp.concatenate([dot(low, extra).astype(BF16), dot(high, extra).astype(BF16)], 1),
        ],
        0,
    )
    gate_part = dot(inputs, wg_ref[...])
    upward = dot(inputs, wu_ref[...])
    hidden = (gate_part / (1.0 + jnp.exp(-gate_part)) * upward).astype(BF16)
    produced = dot(hidden, wd_ref[...]).astype(BF16)
    o_ref[:, :width] = produced[:rows]
    rt = iota((rows, half_rows), 0)
    ct = iota((rows, half_rows), 1)
    target = ct // 4 * 8 + ct % 4
    low_t = jnp.where(rt == target, 1.0, 0.0).astype(BF16)
    high_t = jnp.where(rt == target + 4, 1.0, 0.0).astype(BF16)
    o_ref[:, width:] = (dot(low_t, produced[rows:, :half]) + dot(high_t, produced[rows:, half:])).astype(BF16)


def run_expert(y, w_gate, w_up, w_down):
    steps = 4
    whole = lambda shape: pl.BlockSpec(shape, lambda i: tuple(0 for _ in shape), pipeline_mode=pl.Buffered(1))
    tile = pl.BlockSpec((y.shape[0] // steps, y.shape[1]), lambda i: (i, 0))
    return pl.pallas_call(
        expert_kernel,
        grid=(steps,),
        in_specs=[tile, whole(w_gate.shape), whole(w_up.shape), whole(w_down.shape)],
        out_specs=tile,
        out_shape=jax.ShapeDtypeStruct(y.shape, BF16),
        compiler_params=pltpu.CompilerParams(vmem_limit_bytes=52 * 1024 * 1024),
        name="expert_ffn",
    )(y, w_gate, w_up, w_down)


def combine_kernel(r_ref, extra_ref, rank_ref, gate_ref, spot_ref, o_ref, weight_s):
    step = pl.program_id(0)
    n, experts = rank_ref.shape
    rows = r_ref.shape[0]

    @pl.when(step == 0)
    def _():
        spread = jnp.where(iota((experts, rows), 0) == iota((experts, rows), 1) // 8, 1.0, 0.0).astype(BF16)
        gate = gate_ref[...]
        gate_hi = gate.astype(BF16)
        gate_lo = (gate - gate_hi.astype(F32)).astype(BF16)
        rank_e = dot(rank_ref[...].astype(BF16), spread)
        slot = (iota(rank_e.shape, 1) % 8).astype(F32)
        main = rank_e == slot
        low = (rank_e == slot + 8.0) & (slot < 4.0)
        high = (rank_e == slot + 4.0) & (slot >= 4.0)
        for part, gates in enumerate((gate_hi, gate_lo)):
            spread_gate = dot(gates, spread)
            lines = slice(part * n, (part + 1) * n)
            chosen = jnp.where(main, spread_gate, 0.0).astype(BF16)
            weight_s[0, lines, :rows] = chosen
            weight_s[1, lines, :rows] = chosen
            weight_s[0, lines, rows:] = jnp.where(low, spread_gate, 0.0).astype(BF16)
            weight_s[1, lines, rows:] = jnp.where(high, spread_gate, 0.0).astype(BF16)

    both = weight_s[step // (pl.num_programs(0) // 2)]
    merged = dot(both[:, :rows], r_ref[...]) + dot(both[:, rows:], extra_ref[...])
    merged = merged[:n] + merged[n:]
    parts = o_ref.shape[1]
    w = merged.shape[1] // parts
    spot = spot_ref[...]
    lane = iota(spot.shape, 1)
    big = jnp.floor(spot * (1.0 / 16.0))
    tail = jnp.where(lane == 0, big, jnp.where(lane == 1, spot - 16.0 * big, 0.0))
    tail = tail.reshape(n // 8, 8, 128).astype(BF16)
    for h in range(parts):
        o_ref[:, h, :, :w] = merged[:, h * w : (h + 1) * w].reshape(n // 8, 8, w).astype(BF16)
        o_ref[:, h, :, w:] = tail


def combine(r, rank, gate, spot):
    steps = 4
    n = rank.shape[0]
    width = r.shape[1] * 2 // 3
    rows = r.shape[0]
    whole = lambda shape: pl.BlockSpec(shape, lambda i: tuple(0 for _ in shape))
    return pl.pallas_call(
        combine_kernel,
        grid=(steps,),
        in_specs=[
            pl.BlockSpec((rows, width // steps), lambda i: (0, i)),
            pl.BlockSpec((rows, width // steps), lambda i: (0, steps + i % (steps // 2))),
            whole((n, 128)),
            whole((n, 128)),
            whole((n, 128)),
        ],
        out_specs=pl.BlockSpec((n // 8, 8 // steps, 8, width // 8 + 128), lambda i: (0, i, 0, 0)),
        out_shape=jax.ShapeDtypeStruct((n // 8, 8, 8, width // 8 + 128), BF16),
        scratch_shapes=[VMEM((2, 2 * n, 2 * rows), BF16)],
        compiler_params=pltpu.CompilerParams(vmem_limit_bytes=40 * 1024 * 1024),
        name="combine_rows",
    )(r, r, rank, gate, spot)


def join_kernel(landed_ref, stream_ref, o_ref):
    tokens, w = stream_ref.shape
    tail = landed_ref[:, w:].astype(F32)
    spot = tail[:, 0:1] * 16.0 + tail[:, 1:2]
    count = landed_ref.shape[0]
    hit = jnp.where(spot == iota((count, tokens), 1).astype(F32), 1.0, 0.0).astype(BF16)
    added = lax.dot_general(hit, landed_ref[:, :w], (((0,), (0,)), ((), ())), preferred_element_type=F32)
    o_ref[...] = (stream_ref[...].astype(F32) + added).astype(BF16)


def join(landed, stream):
    return pl.pallas_call(
        join_kernel,
        out_shape=jax.ShapeDtypeStruct(stream.shape, BF16),
        compiler_params=pltpu.CompilerParams(vmem_limit_bytes=40 * 1024 * 1024),
        name="join_rows",
    )(landed, stream)


def qkv_kernel(place_ref, *refs):
    x_refs = refs[:8]
    gain_ref, wq_ref, wk_ref, wv_ref, qg_ref, kg_ref, cos_ref, sin_ref, q_ref, kv_ref, norm_s = refs[8:]
    z = place_ref[1]
    core = place_ref[2]
    tokens, w = x_refs[0].shape
    width = 8 * w
    square = jnp.zeros((tokens, 1), F32)
    for x_ref in x_refs:
        x = x_ref[...].astype(F32)
        square = square + jnp.sum(x * x, 1, keepdims=True)
    scale = lax.rsqrt(square * (1.0 / width) + EPSILON)
    half = tokens // 2
    start = pl.multiple_of(core * half, half)
    for i, x_ref in enumerate(x_refs):
        block = 2 * lax.rem(z + 4 - i % 4, 4) + (core if i < 4 else 1 - core)
        norm = (x_ref[...].astype(F32) * scale * gain_ref[pl.ds(block, 1), :]).astype(BF16)
        norm_s[:, pl.ds(pl.multiple_of(block * w, w), w)] = norm
    queries = dot(norm_s[...], wq_ref[...])
    mine = norm_s[pl.ds(start, half), :]
    keys = dot(mine, wk_ref[...])
    values = dot(mine, wv_ref[...])
    cos = cos_ref[...]
    sin = sin_ref[...]

    def finished(vectors, gains, cos, sin):
        mean = jnp.mean(vectors * vectors, -1, keepdims=True)
        vectors = vectors * lax.rsqrt(mean + EPSILON) * gains
        return vectors * cos + pltpu.roll(vectors, HD // 2, 1) * sin

    factor = math.log2(math.e) / math.sqrt(HD)
    for h in range(q_ref.shape[0]):
        part = slice(h * HD, (h + 1) * HD)
        q_ref[h] = (finished(queries[:, part], qg_ref[:, part], cos, sin) * factor).astype(BF16)
    cos_k = cos_ref[pl.ds(start, half), :]
    sin_k = sin_ref[pl.ds(start, half), :]
    kv_ref[:, :HD] = finished(keys, kg_ref[...], cos_k, sin_k).astype(BF16)
    kv_ref[:, HD:] = values.astype(BF16)


def project(place, blocks, attn_gain, w_query, w_key, w_value, q_gain, k_gain, cos, sin):
    tokens, w = blocks[0].shape
    heads = w_query.shape[1] // HD
    whole = lambda shape: pl.BlockSpec(shape, lambda i, s: tuple(0 for _ in shape))
    column = lambda shape: pl.BlockSpec((shape[0], HD), lambda i, s: (0, s[1]))
    return pl.pallas_call(
        qkv_kernel,
        grid_spec=pltpu.PrefetchScalarGridSpec(
            num_scalar_prefetch=1,
            grid=(1,),
            in_specs=[whole((tokens, w))] * 8
            + [
                whole((8, w)),
                whole(w_query.shape),
                column(w_key.shape),
                column(w_value.shape),
                whole((1, heads * HD)),
                column((1, HD)),
                whole((tokens, HD)),
                whole((tokens, HD)),
            ],
            out_specs=[whole((heads, tokens, HD)), whole((tokens // 2, 2 * HD))],
            scratch_shapes=[VMEM((tokens, 8 * w), BF16)],
        ),
        out_shape=[
            jax.ShapeDtypeStruct((heads, tokens, HD), BF16),
            jax.ShapeDtypeStruct((tokens // 2, 2 * HD), BF16),
        ],
        compiler_params=pltpu.CompilerParams(vmem_limit_bytes=48 * 1024 * 1024),
        name="project_qkv",
    )(
        place,
        *blocks,
        attn_gain.reshape(8, w),
        w_query,
        w_key,
        w_value,
        q_gain.reshape(1, -1),
        k_gain.reshape(1, -1),
        cos,
        sin,
    )


def attend_kernel(place_ref, q_ref, kv_ref, o_ref):
    ctx = place_ref[0]
    core = place_ref[2]
    tokens = q_ref.shape[1]
    shard = kv_ref.shape[1]
    group = 4
    span = group * shard
    q = q_ref[0]

    def fold(carry, chunk, masked):
        highest, totals, weighted = carry
        piece = kv_ref[pl.ds(chunk * group, group)].reshape(span, 2 * HD)
        scores = dot_t(q, piece[:, :HD])
        if masked:
            t = iota((tokens, span), 1)
            key_pos = (chunk * group + t // shard) * (2 * shard) + core * shard + t % shard
            query_pos = ctx * tokens + iota((tokens, span), 0)
            scores = jnp.where(query_pos >= key_pos, scores, NEG)
        fresh = jnp.maximum(highest, jnp.max(scores, 1, keepdims=True))
        weights = jnp.exp2(scores - fresh)
        if masked:
            weights = jnp.where(query_pos >= key_pos, weights, 0.0)
        fade = jnp.exp2(highest - fresh)
        totals = totals * fade + jnp.sum(weights, 1, keepdims=True)
        weighted = weighted * fade + dot(weights.astype(BF16), piece[:, HD:])
        return fresh, totals, weighted

    start = (jnp.full((tokens, 1), NEG, F32), jnp.zeros((tokens, 1), F32), jnp.zeros((tokens, HD), F32))
    whole = ctx // group
    state = lax.fori_loop(0, whole, lambda j, carry: fold(carry, j, False), start)
    highest, totals, weighted = fold(state, whole, True)
    o_ref[0, :, :HD] = weighted
    lane = iota((tokens, HD), 1)
    o_ref[0, :, HD:] = jnp.where(lane < HD // 2, highest, totals)


def attend(place, queries, kv):
    heads, tokens, _ = queries.shape
    return pl.pallas_call(
        attend_kernel,
        grid_spec=pltpu.PrefetchScalarGridSpec(
            num_scalar_prefetch=1,
            grid=(heads,),
            in_specs=[
                pl.BlockSpec((1, tokens, HD), lambda i, s: (i, 0, 0)),
                pl.BlockSpec(kv.shape, lambda i, s: (0, 0, 0)),
            ],
            out_specs=pl.BlockSpec((1, tokens, 2 * HD), lambda i, s: (i, 0, 0)),
        ),
        out_shape=jax.ShapeDtypeStruct((heads, tokens, 2 * HD), F32),
        compiler_params=pltpu.CompilerParams(vmem_limit_bytes=48 * 1024 * 1024),
        name="attend",
    )(place, queries, kv)


def output_kernel(place_ref, own_ref, other_ref, w_ref, o_ref, att_s):
    @pl.when(pl.program_id(0) == 0)
    def _():
        for h in range(own_ref.shape[0]):
            m0 = own_ref[h, :, HD : HD + 1]
            m1 = other_ref[h, :, HD : HD + 1]
            top = jnp.maximum(m0, m1)
            e0 = jnp.exp2(m0 - top)
            e1 = jnp.exp2(m1 - top)
            total = own_ref[h, :, 2 * HD - 1 :] * e0 + other_ref[h, :, 2 * HD - 1 :] * e1
            value = (own_ref[h, :, :HD] * e0 + other_ref[h, :, :HD] * e1) / total
            att_s[:, h * HD : (h + 1) * HD] = value.astype(BF16)

    o_ref[0] = dot(att_s[...], w_ref[...]).astype(BF16)


def project_out(place, own, other, w_out):
    heads, tokens, _ = own.shape
    w = w_out.shape[1] // 8
    whole = pl.BlockSpec((heads, tokens, 2 * HD), lambda i, s: (0, 0, 0))
    return pl.pallas_call(
        output_kernel,
        grid_spec=pltpu.PrefetchScalarGridSpec(
            num_scalar_prefetch=1,
            grid=(8,),
            in_specs=[
                whole,
                whole,
                pl.BlockSpec((heads * HD, w), lambda i, s: (0, 2 * (i % 4) + jnp.where(i < 4, 1 - s[2], s[2]))),
            ],
            out_specs=pl.BlockSpec((1, tokens, w), lambda i, s: (i, 0, 0)),
            scratch_shapes=[VMEM((tokens, heads * HD), BF16)],
        ),
        out_shape=jax.ShapeDtypeStruct((8, tokens, w), BF16),
        compiler_params=pltpu.CompilerParams(vmem_limit_bytes=48 * 1024 * 1024),
        name="project_out",
    )(place, own, other, w_out)


def body(
    branch_rows,
    expert_ids,
    targets,
    router,
    w_gate,
    w_up,
    w_down,
    stream,
    attn_gain,
    q_gain,
    k_gain,
    w_query,
    w_key,
    w_value,
    w_out,
):
    ctx = lax.axis_index("ctx")
    head = lax.axis_index("head")
    z = head // 2
    core = head % 2
    place = jnp.stack([ctx, z, core]).astype(jnp.int32)
    experts = router.shape[1]
    tokens, w = stream.shape
    partner = [(i, i ^ 1) for i in range(8)]

    def along(shard, hops):
        return lax.ppermute(shard, "head", [(i, (i + 2 * hops) % 8) for i in range(8)])

    def everywhere(blocks):
        return lax.all_to_all(blocks, ("ctx", "head"), split_axis=0, concat_axis=0, tiled=True)

    outgoing, rank, gate, spot = dispatch(branch_rows, expert_ids, targets, router)
    shape = (experts, 8, outgoing.shape[1])
    arrived = everywhere(outgoing.reshape(shape)).reshape(outgoing.shape)
    produced = run_expert(arrived, w_gate[0], w_up[0], w_down[0])
    returned = everywhere(produced.reshape(shape)).reshape(outgoing.shape)
    parcels = combine(returned, rank, gate, spot)
    landed = everywhere(parcels.reshape(experts, 8, parcels.shape[3])).reshape(experts * 8, parcels.shape[3])
    joined = join(landed, stream)

    mine = [joined] + [along(joined, hops) for hops in (1, 2, 3)]
    blocks = mine + [lax.ppermute(block, "head", partner) for block in mine]

    half_dim = HD // 2
    frequency = jnp.power(jnp.float32(THETA), -jnp.arange(half_dim, dtype=F32) * 2.0 / HD)
    positions = ctx * tokens + jnp.arange(tokens, dtype=jnp.int32)
    angles = positions.astype(F32)[:, None] * frequency[None, :]
    cosines = jnp.cos(angles)
    sines = jnp.sin(angles)
    cos = jnp.concatenate([cosines, cosines], 1)
    sin = jnp.concatenate([-sines, sines], 1)

    queries, kv = project(place, blocks, attn_gain, w_query, w_key, w_value, q_gain, k_gain, cos, sin)
    all_kv = lax.all_to_all(
        jnp.broadcast_to(kv[None], (16, *kv.shape)), "ctx", split_axis=0, concat_axis=0, tiled=True
    )
    other_queries = lax.ppermute(queries, "head", partner)
    folded = attend(place, jnp.concatenate([queries, other_queries], 0), all_kv)
    heads = queries.shape[0]
    from_partner = lax.ppermute(folded[heads:], "head", partner)
    out = project_out(place, folded[:heads], from_partner, w_out)
    pair = out[4:].astype(F32) + lax.ppermute(out[:4], "head", partner).astype(F32)
    pair = pair.astype(BF16)
    total = lax.dynamic_index_in_dim(pair, z, 0, keepdims=False).astype(F32)
    for hops in (1, 2, 3):
        sent = lax.dynamic_index_in_dim(pair, (z + hops) % 4, 0, keepdims=False)
        total = total + along(sent, hops).astype(F32)
    return (joined.astype(F32) + total).astype(BF16)


def solution(mesh):
    in_specs = (
        P(("ctx", "head"), None),
        P(("ctx", "head"), None),
        P(("ctx", "head")),
        P(),
        P(("ctx", "head"), None, None),
        P(("ctx", "head"), None, None),
        P(("ctx", "head"), None, None),
        P("ctx", "head"),
        P(),
        P("head"),
        P(),
        P(None, "head"),
        P(),
        P(),
        P("head", None),
    )
    out_specs = P("ctx", "head")
    return jax.shard_map(body, mesh=mesh, in_specs=in_specs, out_specs=out_specs, check_vma=False)
```

```python
import math

import jax
import jax.numpy as jnp
from jax import lax
from jax.experimental import pallas as pl
from jax.experimental.pallas import tpu as pltpu
from jax.sharding import PartitionSpec as P

QH = 32
KVH = 4
HD = 128
EPSILON = 1e-06
THETA = 1000000.0
F32 = jnp.float32
BF16 = jnp.bfloat16
VMEM = pltpu.VMEM
NEG = -1e30
MIB = 1024 * 1024


def iota(shape, dim):
    return lax.broadcasted_iota(jnp.int32, shape, dim)


def dot(a, b):
    return jnp.dot(a, b, preferred_element_type=F32)


def dot_t(a, b):
    return lax.dot_general(a, b, (((1,), (1,)), ((), ())), preferred_element_type=F32)


def dispatch_kernel(rows_ref, ids_ref, targets_ref, router_ref, y_ref, rank_ref, gate_ref, spot_ref):
    n, width = rows_ref.shape
    experts = router_ref.shape[1]
    first = iota((n, n), 0)
    second = iota((n, n), 1)
    owner = jnp.broadcast_to((targets_ref[...] // 512).astype(F32), (n, n))
    same = jnp.where((owner.T == owner) & (first < second), 1.0, 0.0)
    place = owner[0:1] * 8.0 + jnp.sum(same, 0, keepdims=True)
    perm = jnp.where(first.astype(F32) == place, 1.0, 0.0)
    spot = (targets_ref[...] % 512).astype(F32)
    spot_ref[...] = jnp.broadcast_to(jnp.sum(perm * spot, 1, keepdims=True), (n, 128))
    perm = perm.astype(BF16)
    rows = dot(perm, rows_ref[...]).astype(BF16)
    ids = dot_t(ids_ref[...].astype(F32).astype(BF16), perm)
    expert = iota((experts, n), 0).astype(F32)
    member = jnp.zeros((experts, n), F32)
    for k in range(ids.shape[0]):
        member = member + jnp.where(expert == ids[k : k + 1, :], 1.0, 0.0)
    before = jnp.where(first < second, 1.0, 0.0).astype(BF16)
    rank = jnp.where(member > 0.5, dot(member.astype(BF16), before), -1.0)
    half = width // 2
    blk = 32
    packed = rank.astype(BF16)
    for i in range(experts // blk):
        spread = jnp.where(iota((blk * 8, experts), 0) // 8 + i * blk == iota((blk * 8, experts), 1), 1.0, 0.0)
        rank_e = dot(spread.astype(BF16), packed)
        slot = (iota(rank_e.shape, 0) % 8).astype(F32)
        main = jnp.where(rank_e == slot, 1.0, 0.0).astype(BF16)
        low = jnp.where((rank_e == slot + 8.0) & (slot < 4.0), 1.0, 0.0).astype(BF16)
        high = jnp.where((rank_e == slot + 4.0) & (slot >= 4.0), 1.0, 0.0).astype(BF16)
        lines = slice(i * blk * 8, (i + 1) * blk * 8)
        y_ref[lines, :width] = dot(main, rows).astype(BF16)
        y_ref[lines, width:] = (dot(low, rows[:, :half]) + dot(high, rows[:, half:])).astype(BF16)
    rank_ref[...] = rank.T
    member_q = member.T > 0.5
    logits = dot(rows, router_ref[...])
    highest = jnp.max(jnp.where(member_q, logits, NEG), 1, keepdims=True)
    raised = jnp.where(member_q, jnp.exp(jnp.minimum(logits - highest, 0.0)), 0.0)
    gate_ref[...] = raised / jnp.sum(raised, 1, keepdims=True)


def dispatch(rows, ids, targets, router):
    n, width = rows.shape
    table = jax.ShapeDtypeStruct((n, 128), F32)
    return pl.pallas_call(
        dispatch_kernel,
        out_shape=[jax.ShapeDtypeStruct((1024, width * 3 // 2), BF16), table, table, table],
        compiler_params=pltpu.CompilerParams(vmem_limit_bytes=16 * MIB),
        name="dispatch_rows",
    )(rows, ids.T, targets.reshape(1, n), router)


def expert_kernel(y_ref, wg_ref, wu_ref, wd_ref, o_ref):
    rows = 256
    half_rows = rows // 2
    width = wg_ref.shape[0]
    half = width // 2
    r = iota((half_rows, rows), 0)
    col = iota((half_rows, rows), 1)
    source = r // 4 * 8 + r % 4
    low = jnp.where(col == source, 1.0, 0.0).astype(BF16)
    high = jnp.where(col == source + 4, 1.0, 0.0).astype(BF16)
    rt = iota((rows, half_rows), 0)
    ct = iota((rows, half_rows), 1)
    target = ct // 4 * 8 + ct % 4
    low_t = jnp.where(rt == target, 1.0, 0.0).astype(BF16)
    high_t = jnp.where(rt == target + 4, 1.0, 0.0).astype(BF16)
    for i in range(y_ref.shape[0] // rows):
        lines = slice(i * rows, (i + 1) * rows)
        extra = y_ref[lines, width:]
        inputs = jnp.concatenate(
            [
                y_ref[lines, :width],
                jnp.concatenate([dot(low, extra).astype(BF16), dot(high, extra).astype(BF16)], 1),
            ],
            0,
        )
        gate_part = dot(inputs, wg_ref[...])
        upward = dot(inputs, wu_ref[...])
        hidden = (gate_part / (1.0 + jnp.exp(-gate_part)) * upward).astype(BF16)
        produced = dot(hidden, wd_ref[...]).astype(BF16)
        o_ref[lines, :width] = produced[:rows]
        o_ref[lines, width:] = (dot(low_t, produced[rows:, :half]) + dot(high_t, produced[rows:, half:])).astype(BF16)


def run_expert(y, w_gate, w_up, w_down):
    return pl.pallas_call(
        expert_kernel,
        out_shape=jax.ShapeDtypeStruct(y.shape, BF16),
        compiler_params=pltpu.CompilerParams(vmem_limit_bytes=16 * MIB),
        name="expert_ffn",
    )(y, w_gate, w_up, w_down)


def combine_kernel(r_ref, rank_ref, gate_ref, spot_ref, o_ref):
    n, experts = rank_ref.shape
    rows = r_ref.shape[0]
    width = r_ref.shape[1] * 2 // 3
    spread = jnp.where(iota((experts, rows), 0) == iota((experts, rows), 1) // 8, 1.0, 0.0).astype(BF16)
    gate = gate_ref[...]
    gate_hi = gate.astype(BF16)
    gate_lo = (gate - gate_hi.astype(F32)).astype(BF16)
    rank_e = dot(rank_ref[...].astype(BF16), spread)
    slot = (iota(rank_e.shape, 1) % 8).astype(F32)
    gates = [dot(gate_hi, spread), dot(gate_lo, spread)]

    def chosen(mask):
        return jnp.concatenate([jnp.where(mask, g, 0.0).astype(BF16) for g in gates], 0)

    main = chosen(rank_e == slot)
    extras = [chosen((rank_e == slot + 8.0) & (slot < 4.0)), chosen((rank_e == slot + 4.0) & (slot >= 4.0))]
    spot = spot_ref[...]
    lane = iota(spot.shape, 1)
    big = jnp.floor(spot * (1.0 / 16.0))
    tail = jnp.where(lane == 0, big, jnp.where(lane == 1, spot - 16.0 * big, 0.0))
    tail = tail.reshape(n // 8, 8, 128).astype(BF16)
    parts = o_ref.shape[1]
    w = width // parts
    span = width // 4
    for c in range(4):
        lines = slice(c * span, (c + 1) * span)
        more = width + (c % 2) * span
        merged = dot(main, r_ref[:, lines]) + dot(extras[c // 2], r_ref[:, more : more + span])
        merged = merged[:n] + merged[n:]
        for i in range(span // w):
            o_ref[:, c * (span // w) + i, :, :w] = merged[:, i * w : (i + 1) * w].reshape(n // 8, 8, w).astype(BF16)
    for h in range(parts):
        o_ref[:, h, :, w:] = tail


def combine(r, rank, gate, spot):
    n = rank.shape[0]
    width = r.shape[1] * 2 // 3
    return pl.pallas_call(
        combine_kernel,
        out_shape=jax.ShapeDtypeStruct((n // 8, 8, 8, width // 8 + 128), BF16),
        compiler_params=pltpu.CompilerParams(vmem_limit_bytes=16 * MIB),
        name="combine_rows",
    )(r, rank, gate, spot)


def join_kernel(landed_ref, stream_ref, o_ref):
    tokens, w = stream_ref.shape
    tail = landed_ref[:, w:].astype(F32)
    spot = tail[:, 0:1] * 16.0 + tail[:, 1:2]
    count = landed_ref.shape[0]
    hit = jnp.where(spot == iota((count, tokens), 1).astype(F32), 1.0, 0.0).astype(BF16)
    added = lax.dot_general(hit, landed_ref[:, :w], (((0,), (0,)), ((), ())), preferred_element_type=F32)
    o_ref[...] = (stream_ref[...].astype(F32) + added).astype(BF16)


def join(landed, stream):
    return pl.pallas_call(
        join_kernel,
        out_shape=jax.ShapeDtypeStruct(stream.shape, BF16),
        compiler_params=pltpu.CompilerParams(vmem_limit_bytes=16 * MIB),
        name="join_rows",
    )(landed, stream)


def qkv_kernel(place_ref, *refs):
    x_refs = refs[:8]
    gain_ref, wq_ref, wkv_ref, qg_ref, kg_ref, cos_ref, sin_ref, low_ref, high_ref, kv_ref, norm_s = refs[8:]
    z = place_ref[1]
    core = place_ref[2]
    tokens, w = x_refs[0].shape
    width = 8 * w
    square = jnp.zeros((tokens, 1), F32)
    for x_ref in x_refs:
        x = x_ref[...].astype(F32)
        square = square + jnp.sum(x * x, 1, keepdims=True)
    scale = lax.rsqrt(square * (1.0 / width) + EPSILON)
    half = tokens // 2
    start = pl.multiple_of(core * half, half)
    for i, x_ref in enumerate(x_refs):
        block = 2 * lax.rem(z + 4 - i % 4, 4) + (core if i < 4 else 1 - core)
        norm = (x_ref[...].astype(F32) * scale * gain_ref[pl.ds(block, 1), :]).astype(BF16)
        norm_s[:, pl.ds(pl.multiple_of(block * w, w), w)] = norm
    both = dot(norm_s[pl.ds(start, half), :], wkv_ref[...])
    queries = dot(norm_s[...], wq_ref[...])

    def finished(vectors, gains, cos, sin):
        mean = jnp.mean(vectors * vectors, -1, keepdims=True)
        vectors = vectors * lax.rsqrt(mean + EPSILON) * gains
        return vectors * cos + pltpu.roll(vectors, HD // 2, 1) * sin

    cos_k = cos_ref[pl.ds(start, half), :]
    sin_k = sin_ref[pl.ds(start, half), :]
    kv_ref[:, :HD] = finished(both[:, :HD], kg_ref[...], cos_k, sin_k).astype(BF16)
    kv_ref[:, HD:] = both[:, HD:].astype(BF16)
    factor = math.log2(math.e) / math.sqrt(HD)
    cos = cos_ref[...]
    sin = sin_ref[...]
    for h in range(low_ref.shape[0]):
        part = slice(h * HD, (h + 1) * HD)
        done = (finished(queries[:, part], qg_ref[:, part], cos, sin) * factor).astype(BF16)
        low_ref[h] = done[:half]
        high_ref[h] = done[half:]


def project(place, blocks, row_gain, w_query, w_kv, q_gain, key_gain, cos, sin):
    tokens, w = blocks[0].shape
    heads = w_query.shape[1] // HD
    part = jax.ShapeDtypeStruct((heads, tokens // 2, HD), BF16)
    return pl.pallas_call(
        qkv_kernel,
        in_specs=[pl.BlockSpec(memory_space=pltpu.SMEM)] + [pl.BlockSpec(memory_space=VMEM)] * 15,
        out_shape=[part, part, jax.ShapeDtypeStruct((tokens // 2, 2 * HD), BF16)],
        scratch_shapes=[VMEM((tokens, 8 * w), BF16)],
        compiler_params=pltpu.CompilerParams(vmem_limit_bytes=20 * MIB),
        name="project_qkv",
    )(
        place,
        *blocks,
        row_gain,
        w_query,
        w_kv,
        q_gain.reshape(1, -1),
        key_gain,
        cos,
        sin,
    )


def attend_kernel(place_ref, low_ref, high_ref, kv_ref, o_ref, value_s):
    core = place_ref[2]
    shards, shard, _ = kv_ref.shape
    heads, half, _ = low_ref.shape
    group = 4
    subs = 2
    span = group * shard
    rows = heads * half // subs
    value_s[:, :, :HD] = kv_ref[:, :, HD:]
    value_s[:, :, HD:] = jnp.ones((shards, shard, HD), BF16)

    for upper, q_ref in enumerate((low_ref, high_ref)):
        own = place_ref[0] if upper == 0 else shards - 1 - place_ref[0]
        queries = q_ref[...].reshape(heads * half, HD)
        pieces = [queries[i * rows : (i + 1) * rows] for i in range(subs)]

        def fold(carry, chunk, masked):
            keys = kv_ref[pl.ds(chunk * group, group), :, :HD].reshape(span, HD)
            values = value_s[pl.ds(chunk * group, group)].reshape(span, 2 * HD)
            every = [dot_t(piece, keys) for piece in pieces]
            result = []
            for (highest, weighted), scores in zip(carry, every):
                if masked:
                    t = iota((rows, span), 1)
                    key_pos = (chunk * group + t // shard) * (2 * shard) + core * shard + t % shard
                    query_pos = own * (2 * half) + upper * half + iota((rows, span), 0) % half
                    allowed = query_pos >= key_pos
                    scores = jnp.where(allowed, scores, NEG)
                fresh = jnp.maximum(highest, jnp.max(scores, 1, keepdims=True))
                weights = jnp.exp2(scores - fresh)
                if masked:
                    weights = jnp.where(allowed, weights, 0.0)
                weighted = weighted * jnp.exp2(highest - fresh) + dot(weights.astype(BF16), values)
                result.append((fresh, weighted))
            return tuple(result)

        start = tuple((jnp.full((rows, 1), NEG, F32), jnp.zeros((rows, 2 * HD), F32)) for _ in range(subs))
        whole = own // group
        state = lax.fori_loop(0, whole, lambda j, carry: fold(carry, j, False), start)
        state = fold(state, whole, True)
        lane = iota((rows, HD), 1)
        for i, (highest, weighted) in enumerate(state):
            part = slice(i * (heads // subs), (i + 1) * (heads // subs))
            o_ref[part, upper * half : (upper + 1) * half, :HD] = weighted[:, :HD].reshape(heads // subs, half, HD)
            stats = jnp.where(lane < HD // 2, highest, weighted[:, HD:])
            o_ref[part, upper * half : (upper + 1) * half, HD:] = stats.reshape(heads // subs, half, HD)


def attend(place, low, high, kv):
    heads, half, _ = low.shape
    return pl.pallas_call(
        attend_kernel,
        in_specs=[pl.BlockSpec(memory_space=pltpu.SMEM)] + [pl.BlockSpec(memory_space=VMEM)] * 3,
        out_shape=jax.ShapeDtypeStruct((heads, 2 * half, 2 * HD), F32),
        scratch_shapes=[VMEM(kv.shape, BF16)],
        compiler_params=pltpu.CompilerParams(vmem_limit_bytes=28 * MIB),
        name="attend",
    )(place, low, high, kv)


def merge_kernel(place_ref, own_ref, other_ref, w_ref, att_ref, o_ref):
    for h in range(own_ref.shape[0]):
        m0 = own_ref[h, :, HD : HD + 1]
        m1 = other_ref[h, :, HD : HD + 1]
        top = jnp.maximum(m0, m1)
        e0 = jnp.exp2(m0 - top)
        e1 = jnp.exp2(m1 - top)
        total = own_ref[h, :, 2 * HD - 1 :] * e0 + other_ref[h, :, 2 * HD - 1 :] * e1
        share = 1.0 / total
        value = own_ref[h, :, :HD] * (e0 * share) + other_ref[h, :, :HD] * (e1 * share)
        att_ref[:, h * HD : (h + 1) * HD] = value.astype(BF16)
    project_blocks(place_ref[1], 1 - place_ref[2], att_ref, w_ref, o_ref)


def project_blocks(z, core, att_ref, w_ref, o_ref):
    w = o_ref.shape[2]
    for i in range(o_ref.shape[0]):
        block = 2 * lax.rem(z + i, 4) + core
        o_ref[i] = dot(att_ref[...], w_ref[:, pl.ds(pl.multiple_of(block * w, w), w)]).astype(BF16)


def own_kernel(place_ref, att_ref, w_ref, o_ref):
    project_blocks(place_ref[1], place_ref[2], att_ref, w_ref, o_ref)


def merge_and_project(place, own, other, w_out):
    heads, tokens, _ = own.shape
    return pl.pallas_call(
        merge_kernel,
        in_specs=[pl.BlockSpec(memory_space=pltpu.SMEM)] + [pl.BlockSpec(memory_space=VMEM)] * 3,
        out_shape=[
            jax.ShapeDtypeStruct((tokens, heads * HD), BF16),
            jax.ShapeDtypeStruct((4, tokens, w_out.shape[1] // 8), BF16),
        ],
        compiler_params=pltpu.CompilerParams(vmem_limit_bytes=16 * MIB),
        name="merge_and_project",
    )(place, own, other, w_out)


def project_own(place, attended, w_out):
    return pl.pallas_call(
        own_kernel,
        in_specs=[pl.BlockSpec(memory_space=pltpu.SMEM)] + [pl.BlockSpec(memory_space=VMEM)] * 2,
        out_shape=jax.ShapeDtypeStruct((4, attended.shape[0], w_out.shape[1] // 8), BF16),
        compiler_params=pltpu.CompilerParams(vmem_limit_bytes=16 * MIB),
        name="project_own",
    )(place, attended, w_out)


def body(
    branch_rows,
    expert_ids,
    targets,
    router,
    w_gate,
    w_up,
    w_down,
    stream,
    attn_gain,
    q_gain,
    k_gain,
    w_query,
    w_key,
    w_value,
    w_out,
):
    ctx = lax.axis_index("ctx")
    head = lax.axis_index("head")
    z = head // 2
    core = head % 2
    place = jnp.stack([ctx, z, core]).astype(jnp.int32)
    experts = router.shape[1]
    tokens, w = stream.shape
    partner = [(i, i ^ 1) for i in range(8)]
    mirror = [(i, 15 - i) for i in range(16)]

    def along(shard, hops):
        return lax.ppermute(shard, "head", [(i, (i + 2 * hops) % 8) for i in range(8)])

    def everywhere(blocks):
        return lax.all_to_all(blocks, ("ctx", "head"), split_axis=0, concat_axis=0, tiled=True)

    half_dim = HD // 2
    frequency = jnp.power(jnp.float32(THETA), -jnp.arange(half_dim, dtype=F32) * 2.0 / HD)
    positions = ctx * tokens + jnp.arange(tokens, dtype=jnp.int32)
    angles = positions.astype(F32)[:, None] * frequency[None, :]
    cosines = jnp.cos(angles)
    sines = jnp.sin(angles)
    cos = jnp.concatenate([cosines, cosines], 1)
    sin = jnp.concatenate([-sines, sines], 1)

    outgoing, rank, gate, spot = dispatch(branch_rows, expert_ids, targets, router)
    shape = (experts, 8, outgoing.shape[1])
    arrived = everywhere(outgoing.reshape(shape)).reshape(outgoing.shape)
    first_column = z * HD
    w_kv = jnp.concatenate([lax.dynamic_slice_in_dim(w, first_column, HD, 1) for w in (w_key, w_value)], 1)
    key_gain = lax.dynamic_slice_in_dim(k_gain, first_column, HD, 0).reshape(1, HD)
    row_gain = attn_gain.reshape(8, w)
    early = (arrived, cos, sin, w_kv, key_gain, row_gain, place)
    arrived, cos, sin, w_kv, key_gain, row_gain, place = lax.optimization_barrier(early)
    produced = run_expert(arrived, w_gate[0], w_up[0], w_down[0])
    returned = everywhere(produced.reshape(shape)).reshape(outgoing.shape)
    parcels = combine(returned, rank, gate, spot)
    landed = everywhere(parcels.reshape(experts, 8, parcels.shape[3])).reshape(experts * 8, parcels.shape[3])
    joined = join(landed, stream)

    mine = [joined] + [along(joined, hops) for hops in (1, 2, 3)]
    blocks = mine + [lax.ppermute(block, "head", partner) for block in mine]
    low, high, kv = project(place, blocks, row_gain, w_query, w_kv, q_gain, key_gain, cos, sin)
    all_kv = lax.all_to_all(
        jnp.broadcast_to(kv[None], (16, *kv.shape)), "ctx", split_axis=0, concat_axis=0, tiled=True
    )
    high = lax.ppermute(high, "ctx", mirror)
    partner_low = lax.ppermute(low, "head", partner)
    partner_high = lax.ppermute(high, "head", partner)
    for_partner = attend(place, partner_low, partner_high, all_kv)
    from_partner = lax.ppermute(for_partner, "head", partner)
    folded = attend(place, low, high, all_kv)
    attended, sent = merge_and_project(place, folded, from_partner, w_out)
    received = lax.ppermute(sent, "head", partner)
    kept = project_own(place, attended, w_out)
    pair = [(kept[i].astype(F32) + received[i].astype(F32)).astype(BF16) for i in range(4)]
    total = pair[0].astype(F32)
    for hops in (1, 2, 3):
        total = total + along(pair[hops], hops).astype(F32)
    half = tokens // 2
    upper = lax.ppermute(total[half:].astype(BF16), "ctx", mirror)
    summed = jnp.concatenate([total[:half], upper.astype(F32)], 0)
    return (joined.astype(F32) + summed).astype(BF16)


def solution(mesh):
    in_specs = (
        P(("ctx", "head"), None),
        P(("ctx", "head"), None),
        P(("ctx", "head")),
        P(),
        P(("ctx", "head"), None, None),
        P(("ctx", "head"), None, None),
        P(("ctx", "head"), None, None),
        P("ctx", "head"),
        P(),
        P("head"),
        P(),
        P(None, "head"),
        P(),
        P(),
        P("head", None),
    )
    out_specs = P("ctx", "head")
    return jax.shard_map(body, mesh=mesh, in_specs=in_specs, out_specs=out_specs, check_vma=False)
```

```python
import math

import jax
import jax.numpy as jnp
import numpy as np
from jax import lax
from jax.experimental import pallas as pl
from jax.experimental.pallas import tpu as pltpu
from jax.sharding import PartitionSpec as P

QH = 32
KVH = 4
HD = 128
EPSILON = 1e-06
THETA = 1000000.0
F32 = jnp.float32
BF16 = jnp.bfloat16
VMEM = pltpu.VMEM
NEG = -1e30
MIB = 1024 * 1024


def iota(shape, dim):
    return lax.broadcasted_iota(jnp.int32, shape, dim)


def dot(a, b):
    return jnp.dot(a, b, preferred_element_type=F32)


def dot_t(a, b):
    return lax.dot_general(a, b, (((1,), (1,)), ((), ())), preferred_element_type=F32)


def start_loads(pairs, sems):
    loads = [pltpu.make_async_copy(source, target, sems.at[i]) for i, (source, target) in enumerate(pairs)]
    for load in loads:
        load.start()
    return loads


def dispatch_kernel(
    rows_hbm, ids_hbm, targets_hbm, router_hbm, y_ref, rank_ref, gate_ref, spot_ref,
    rows_ref, ids_ref, targets_ref, router_ref, sems,
):
    loads = start_loads(
        [(targets_hbm, targets_ref), (ids_hbm, ids_ref), (rows_hbm, rows_ref), (router_hbm, router_ref)], sems
    )
    n, width = rows_ref.shape
    for load in loads[:3]:
        load.wait()
    experts = router_ref.shape[1]
    first = iota((n, n), 0)
    second = iota((n, n), 1)
    owner = jnp.broadcast_to((targets_ref[...] // 512).astype(F32), (n, n))
    same = jnp.where((owner.T == owner) & (first < second), 1.0, 0.0)
    place = owner[0:1] * 8.0 + jnp.sum(same, 0, keepdims=True)
    perm = jnp.where(first.astype(F32) == place, 1.0, 0.0)
    spot = (targets_ref[...] % 512).astype(F32)
    spot_ref[...] = jnp.broadcast_to(jnp.sum(perm * spot, 1, keepdims=True), (n, 128))
    perm = perm.astype(BF16)
    rows = dot(perm, rows_ref[...]).astype(BF16)
    ids = dot_t(ids_ref[...].astype(F32).astype(BF16), perm)
    expert = iota((experts, n), 0).astype(F32)
    member = jnp.zeros((experts, n), F32)
    for k in range(ids.shape[0]):
        member = member + jnp.where(expert == ids[k : k + 1, :], 1.0, 0.0)
    before = jnp.where(first < second, 1.0, 0.0).astype(BF16)
    rank = jnp.where(member > 0.5, dot(member.astype(BF16), before), -1.0)
    half = width // 2
    blk = 32
    packed = rank.astype(BF16)
    for i in range(experts // blk):
        spread = jnp.where(iota((blk * 8, experts), 0) // 8 + i * blk == iota((blk * 8, experts), 1), 1.0, 0.0)
        rank_e = dot(spread.astype(BF16), packed)
        slot = (iota(rank_e.shape, 0) % 8).astype(F32)
        main = jnp.where(rank_e == slot, 1.0, 0.0).astype(BF16)
        low = jnp.where((rank_e == slot + 8.0) & (slot < 4.0), 1.0, 0.0).astype(BF16)
        high = jnp.where((rank_e == slot + 4.0) & (slot >= 4.0), 1.0, 0.0).astype(BF16)
        lines = slice(i * blk * 8, (i + 1) * blk * 8)
        y_ref[lines, :width] = dot(main, rows).astype(BF16)
        y_ref[lines, width:] = (dot(low, rows[:, :half]) + dot(high, rows[:, half:])).astype(BF16)
    rank_ref[...] = rank.T
    member_q = member.T > 0.5
    loads[3].wait()
    logits = dot(rows, router_ref[...])
    highest = jnp.max(jnp.where(member_q, logits, NEG), 1, keepdims=True)
    raised = jnp.where(member_q, jnp.exp(jnp.minimum(logits - highest, 0.0)), 0.0)
    gate_ref[...] = raised / jnp.sum(raised, 1, keepdims=True)


def dispatch(rows, ids, targets, router):
    n, width = rows.shape
    table = jax.ShapeDtypeStruct((n, 128), F32)
    return pl.pallas_call(
        dispatch_kernel,
        in_specs=[pl.BlockSpec(memory_space=pltpu.HBM)] * 4,
        out_shape=[jax.ShapeDtypeStruct((1024, width * 3 // 2), BF16), table, table, table],
        scratch_shapes=[
            VMEM((n, width), BF16),
            VMEM((8, n), jnp.int32),
            VMEM((1, n), jnp.int32),
            VMEM(router.shape, BF16),
            pltpu.SemaphoreType.DMA((4,)),
        ],
        compiler_params=pltpu.CompilerParams(vmem_limit_bytes=16 * MIB),
        name="dispatch_rows",
    )(rows, ids.T, targets.reshape(1, n), router)


def expert_kernel(y_ref, wg_ref, wu_ref, wd_ref, o_ref):
    rows = 256
    half_rows = rows // 2
    width = wg_ref.shape[0]
    half = width // 2
    r = iota((half_rows, rows), 0)
    col = iota((half_rows, rows), 1)
    source = r // 4 * 8 + r % 4
    low = jnp.where(col == source, 1.0, 0.0).astype(BF16)
    high = jnp.where(col == source + 4, 1.0, 0.0).astype(BF16)
    rt = iota((rows, half_rows), 0)
    ct = iota((rows, half_rows), 1)
    target = ct // 4 * 8 + ct % 4
    low_t = jnp.where(rt == target, 1.0, 0.0).astype(BF16)
    high_t = jnp.where(rt == target + 4, 1.0, 0.0).astype(BF16)
    for i in range(y_ref.shape[0] // rows):
        lines = slice(i * rows, (i + 1) * rows)
        extra = y_ref[lines, width:]
        inputs = jnp.concatenate(
            [
                y_ref[lines, :width],
                jnp.concatenate([dot(low, extra).astype(BF16), dot(high, extra).astype(BF16)], 1),
            ],
            0,
        )
        gate_part = dot(inputs, wg_ref[...])
        upward = dot(inputs, wu_ref[...])
        hidden = (gate_part / (1.0 + jnp.exp(-gate_part)) * upward).astype(BF16)
        produced = dot(hidden, wd_ref[...]).astype(BF16)
        o_ref[lines, :width] = produced[:rows]
        o_ref[lines, width:] = (dot(low_t, produced[rows:, :half]) + dot(high_t, produced[rows:, half:])).astype(BF16)


def run_expert(y, w_gate, w_up, w_down):
    return pl.pallas_call(
        expert_kernel,
        out_shape=jax.ShapeDtypeStruct(y.shape, BF16),
        compiler_params=pltpu.CompilerParams(vmem_limit_bytes=16 * MIB),
        name="expert_ffn",
    )(y, w_gate, w_up, w_down)


def combine_kernel(r_ref, rank_ref, gate_ref, spot_ref, o_ref):
    n, experts = rank_ref.shape
    rows = r_ref.shape[0]
    width = r_ref.shape[1] * 2 // 3
    spread = jnp.where(iota((experts, rows), 0) == iota((experts, rows), 1) // 8, 1.0, 0.0).astype(BF16)
    gate = gate_ref[...]
    gate_hi = gate.astype(BF16)
    gate_lo = (gate - gate_hi.astype(F32)).astype(BF16)
    rank_e = dot(rank_ref[...].astype(BF16), spread)
    slot = (iota(rank_e.shape, 1) % 8).astype(F32)
    gates = [dot(gate_hi, spread), dot(gate_lo, spread)]

    def chosen(mask):
        return jnp.concatenate([jnp.where(mask, g, 0.0).astype(BF16) for g in gates], 0)

    main = chosen(rank_e == slot)
    extras = [chosen((rank_e == slot + 8.0) & (slot < 4.0)), chosen((rank_e == slot + 4.0) & (slot >= 4.0))]
    spot = spot_ref[...]
    lane = iota(spot.shape, 1)
    big = jnp.floor(spot * (1.0 / 16.0))
    tail = jnp.where(lane == 0, big, jnp.where(lane == 1, spot - 16.0 * big, 0.0))
    tail = tail.reshape(n // 8, 8, 128).astype(BF16)
    parts = o_ref.shape[1]
    w = width // parts
    span = width // 4
    for c in range(4):
        lines = slice(c * span, (c + 1) * span)
        more = width + (c % 2) * span
        merged = dot(main, r_ref[:, lines]) + dot(extras[c // 2], r_ref[:, more : more + span])
        merged = merged[:n] + merged[n:]
        for i in range(span // w):
            o_ref[:, c * (span // w) + i, :, :w] = merged[:, i * w : (i + 1) * w].reshape(n // 8, 8, w).astype(BF16)
    for h in range(parts):
        o_ref[:, h, :, w:] = tail


def combine(r, rank, gate, spot):
    n = rank.shape[0]
    width = r.shape[1] * 2 // 3
    return pl.pallas_call(
        combine_kernel,
        out_shape=jax.ShapeDtypeStruct((n // 8, 8, 8, width // 8 + 128), BF16),
        compiler_params=pltpu.CompilerParams(vmem_limit_bytes=16 * MIB),
        name="combine_rows",
    )(r, rank, gate, spot)


def join_kernel(landed_ref, stream_ref, keep_ref, give_ref):
    core = lax.rem(lax.axis_index("head"), 2)
    tokens, w = stream_ref.shape
    half = tokens // 2
    tail = landed_ref[:, w:].astype(F32)
    spot = tail[:, 0:1] * 16.0 + tail[:, 1:2]
    count = landed_ref.shape[0]
    hit = jnp.where(spot == iota((count, tokens), 1).astype(F32), 1.0, 0.0).astype(BF16)
    added = lax.dot_general(hit, landed_ref[:, :w], (((0,), (0,)), ((), ())), preferred_element_type=F32)
    joined = stream_ref[...].astype(F32) + added
    keep_ref[...] = jnp.where(core == 0, joined[:half], joined[half:]).astype(BF16)
    give_ref[...] = jnp.where(core == 0, joined[half:], joined[:half]).astype(BF16)


def join(landed, stream):
    part = jax.ShapeDtypeStruct((stream.shape[0] // 2, stream.shape[1]), BF16)
    return pl.pallas_call(
        join_kernel,
        out_shape=[part, part],
        compiler_params=pltpu.CompilerParams(vmem_limit_bytes=16 * MIB),
        name="join_rows",
    )(landed, stream)


def turning_tables(tokens, shards):
    frequency = THETA ** (-np.arange(HD // 2, dtype=np.float64) * 2.0 / HD)

    def table(positions):
        angles = np.asarray(positions, np.float64)[:, None] * np.concatenate([frequency, frequency])[None, :]
        return np.stack([np.cos(angles), np.sin(angles)]).astype(np.float32)

    return table(np.arange(tokens)), table(np.arange(shards) * tokens)


def turned(vectors, gains, near, far, shard):
    mean = jnp.mean(vectors * vectors, -1, keepdims=True)
    vectors = vectors * lax.rsqrt(mean + EPSILON) * gains
    far_cos = far[0][pl.ds(shard, 1), :]
    far_sin = far[1][pl.ds(shard, 1), :]
    cos = near[0] * far_cos - near[1] * far_sin
    sin = near[1] * far_cos + near[0] * far_sin
    sign = jnp.where(iota((1, HD), 1) < HD // 2, -1.0, 1.0)
    return vectors * cos + pltpu.roll(vectors, HD // 2, 1) * (sin * sign)


def keys_kernel(x0, x1, x2, x3, gain_ref, kg_ref, wk_hbm, wv_hbm, near_ref, far_ref, kv_ref, norm_ref, wkv_ref, sems):
    ctx = lax.axis_index("ctx")
    head = lax.axis_index("head")
    z = head // 2
    core = lax.rem(head, 2)
    x_refs = (x0, x1, x2, x3)
    columns = pl.ds(pl.multiple_of(z * HD, HD), HD)
    loads = start_loads(
        [(wk_hbm.at[:, columns], wkv_ref.at[:, :HD]), (wv_hbm.at[:, columns], wkv_ref.at[:, HD:])], sems
    )
    _, half, w = x0.shape
    width = 8 * w
    square = jnp.zeros((half, 1), F32)
    for x_ref in x_refs:
        for j in range(2):
            x = x_ref[j].astype(F32)
            square = square + jnp.sum(x * x, 1, keepdims=True)
    scale = lax.rsqrt(square * (1.0 / width) + EPSILON)
    for i, x_ref in enumerate(x_refs):
        for j in range(2):
            block = 2 * lax.rem(z + 4 - i, 4) + (core if j == 0 else 1 - core)
            norm = (x_ref[j].astype(F32) * scale * gain_ref[:, pl.ds(pl.multiple_of(block * w, w), w)]).astype(BF16)
            norm_ref[:, pl.ds(pl.multiple_of(block * w, w), w)] = norm
    for load in loads:
        load.wait()
    both = dot(norm_ref[...], wkv_ref[...])
    shard = jnp.where(core == 0, ctx, far_ref.shape[1] - 1 - ctx)
    near = [jnp.where(core == 0, near_ref[t, :half], near_ref[t, half:]) for t in range(2)]
    far = [far_ref.at[0], far_ref.at[1]]
    kv_ref[:, :HD] = turned(both[:, :HD], kg_ref[pl.ds(z, 1), :], near, far, shard).astype(BF16)
    kv_ref[:, HD:] = both[:, HD:].astype(BF16)


def project_keys(blocks, row_gain, key_gain, w_key, w_value, near, far):
    _, half, w = blocks[0].shape
    return pl.pallas_call(
        keys_kernel,
        in_specs=[pl.BlockSpec(memory_space=VMEM)] * 6
        + [pl.BlockSpec(memory_space=pltpu.HBM)] * 2
        + [pl.BlockSpec(memory_space=VMEM)] * 2,
        out_shape=[jax.ShapeDtypeStruct((half, 2 * HD), BF16), jax.ShapeDtypeStruct((half, 8 * w), BF16)],
        scratch_shapes=[VMEM((w_key.shape[0], 2 * HD), BF16), pltpu.SemaphoreType.DMA((2,))],
        compiler_params=pltpu.CompilerParams(vmem_limit_bytes=16 * MIB),
        name="project_keys",
    )(*blocks, row_gain, key_gain, w_key, w_value, near, far)


def queries_kernel(own_ref, other_ref, wq_ref, qg_ref, near_ref, far_ref, low_ref, high_ref):
    ctx = lax.axis_index("ctx")
    core = lax.rem(lax.axis_index("head"), 2)
    half = own_ref.shape[0]
    factor = math.log2(math.e) / math.sqrt(HD)
    far = [far_ref.at[0], far_ref.at[1]]
    for upper, o_ref in enumerate((low_ref, high_ref)):
        norm = jnp.where(core == upper, own_ref[...], other_ref[...])
        queries = dot(norm, wq_ref[...])
        shard = ctx if upper == 0 else far_ref.shape[1] - 1 - ctx
        near = [near_ref[t, upper * half : (upper + 1) * half] for t in range(2)]
        for h in range(o_ref.shape[0]):
            part = slice(h * HD, (h + 1) * HD)
            o_ref[h] = (turned(queries[:, part], qg_ref[:, part], near, far, shard) * factor).astype(BF16)


def project_queries(own, other, w_query, q_gain, near, far):
    heads = w_query.shape[1] // HD
    part = jax.ShapeDtypeStruct((heads, own.shape[0], HD), BF16)
    return pl.pallas_call(
        queries_kernel,
        out_shape=[part, part],
        compiler_params=pltpu.CompilerParams(vmem_limit_bytes=16 * MIB),
        name="project_queries",
    )(own, other, w_query, q_gain.reshape(1, -1), near, far)


def attend_kernel(low_ref, high_ref, kv_ref, o_ref, value_s):
    ctx = lax.axis_index("ctx")
    core = lax.rem(lax.axis_index("head"), 2)
    shards, shard, _ = kv_ref.shape
    heads, half, _ = low_ref.shape
    group = 4
    subs = 2
    span = group * shard
    rows = heads * half // subs
    value_s[:, :, :HD] = kv_ref[:, :, HD:]
    value_s[:, :, HD:] = jnp.ones((shards, shard, HD), BF16)

    for upper, q_ref in enumerate((low_ref, high_ref)):
        own = ctx if upper == 0 else shards - 1 - ctx
        queries = q_ref[...].reshape(heads * half, HD)
        pieces = [queries[i * rows : (i + 1) * rows] for i in range(subs)]

        def fold(carry, chunk, masked):
            first = jnp.where(core == 0, chunk, shards // group - 1 - chunk) * group
            keys = kv_ref[pl.ds(first, group), :, :HD].reshape(span, HD)
            values = value_s[pl.ds(first, group)].reshape(span, 2 * HD)
            every = [dot_t(piece, keys) for piece in pieces]
            result = []
            for (highest, weighted), scores in zip(carry, every):
                if masked:
                    t = iota((rows, span), 1)
                    place = first + t // shard
                    key_pos = jnp.where(core == 0, place, shards - 1 - place) * (2 * shard) + core * shard + t % shard
                    query_pos = own * (2 * half) + upper * half + iota((rows, span), 0) % half
                    allowed = query_pos >= key_pos
                    scores = jnp.where(allowed, scores, NEG)
                fresh = jnp.maximum(highest, jnp.max(scores, 1, keepdims=True))
                weights = jnp.exp2(scores - fresh)
                if masked:
                    weights = jnp.where(allowed, weights, 0.0)
                weighted = weighted * jnp.exp2(highest - fresh) + dot(weights.astype(BF16), values)
                result.append((fresh, weighted))
            return tuple(result)

        start = tuple((jnp.full((rows, 1), NEG, F32), jnp.zeros((rows, 2 * HD), F32)) for _ in range(subs))
        whole = own // group
        state = lax.fori_loop(0, whole, lambda j, carry: fold(carry, j, False), start)
        state = fold(state, whole, True)
        lane = iota((rows, HD), 1)
        for i, (highest, weighted) in enumerate(state):
            part = slice(i * (heads // subs), (i + 1) * (heads // subs))
            o_ref[part, upper * half : (upper + 1) * half, :HD] = weighted[:, :HD].reshape(heads // subs, half, HD)
            stats = jnp.where(lane < HD // 2, highest, weighted[:, HD:])
            o_ref[part, upper * half : (upper + 1) * half, HD:] = stats.reshape(heads // subs, half, HD)


def attend(low, high, kv):
    heads, half, _ = low.shape
    return pl.pallas_call(
        attend_kernel,
        out_shape=jax.ShapeDtypeStruct((heads, 2 * half, 2 * HD), F32),
        scratch_shapes=[VMEM(kv.shape, BF16)],
        compiler_params=pltpu.CompilerParams(vmem_limit_bytes=28 * MIB),
        name="attend",
    )(low, high, kv)


def project_blocks(attended, core, w_ref, o_ref):
    z = lax.axis_index("head") // 2
    w = o_ref.shape[3]
    for i in range(o_ref.shape[0]):
        for j in range(2):
            block = 2 * lax.rem(z + i, 4) + (core if j == 0 else 1 - core)
            o_ref[i, j] = dot(attended, w_ref[:, pl.ds(pl.multiple_of(block * w, w), w)]).astype(BF16)


def merge_kernel(own_ref, other_ref, w_ref, keep_ref, o_ref):
    core = lax.rem(lax.axis_index("head"), 2)
    half = keep_ref.shape[0]
    given = []
    for h in range(own_ref.shape[0]):
        m0 = own_ref[h, :, HD : HD + 1]
        m1 = other_ref[h, :, HD : HD + 1]
        top = jnp.maximum(m0, m1)
        e0 = jnp.exp2(m0 - top)
        e1 = jnp.exp2(m1 - top)
        total = own_ref[h, :, 2 * HD - 1 :] * e0 + other_ref[h, :, 2 * HD - 1 :] * e1
        share = 1.0 / total
        value = own_ref[h, :, :HD] * (e0 * share) + other_ref[h, :, :HD] * (e1 * share)
        keep_ref[:, h * HD : (h + 1) * HD] = jnp.where(core == 0, value[:half], value[half:]).astype(BF16)
        given.append(jnp.where(core == 0, value[half:], value[:half]).astype(BF16))
    project_blocks(jnp.concatenate(given, 1), 1 - core, w_ref, o_ref)


def own_kernel(attended_ref, w_ref, o_ref):
    project_blocks(attended_ref[...], lax.rem(lax.axis_index("head"), 2), w_ref, o_ref)


def merge_and_project(own, other, w_out):
    heads, tokens, _ = own.shape
    return pl.pallas_call(
        merge_kernel,
        out_shape=[
            jax.ShapeDtypeStruct((tokens // 2, heads * HD), BF16),
            jax.ShapeDtypeStruct((4, 2, tokens // 2, w_out.shape[1] // 8), BF16),
        ],
        compiler_params=pltpu.CompilerParams(vmem_limit_bytes=16 * MIB),
        name="merge_and_project",
    )(own, other, w_out)


def project_own(attended, w_out):
    return pl.pallas_call(
        own_kernel,
        out_shape=jax.ShapeDtypeStruct((4, 2, attended.shape[0], w_out.shape[1] // 8), BF16),
        compiler_params=pltpu.CompilerParams(vmem_limit_bytes=16 * MIB),
        name="project_own",
    )(attended, w_out)


def body(
    branch_rows,
    expert_ids,
    targets,
    router,
    w_gate,
    w_up,
    w_down,
    stream,
    attn_gain,
    q_gain,
    k_gain,
    w_query,
    w_key,
    w_value,
    w_out,
):
    core = lax.axis_index("head") % 2
    experts = router.shape[1]
    tokens, w = stream.shape
    partner = [(i, i ^ 1) for i in range(8)]

    def to_partner(shard):
        return lax.ppermute(shard, "head", partner)

    def along(shard, hops):
        pairs = []
        for c in range(16):
            for h in range(8):
                there = c if h % 2 == 0 else 15 - c
                pairs.append((c * 8 + h, there * 8 + (h + 2 * hops) % 8))
        return lax.ppermute(shard, ("ctx", "head"), pairs)

    def everywhere(blocks):
        return lax.all_to_all(blocks, ("ctx", "head"), split_axis=0, concat_axis=0, tiled=True)

    outgoing, rank, gate, spot = dispatch(branch_rows, expert_ids, targets, router)
    shape = (experts, 8, outgoing.shape[1])
    arrived = everywhere(outgoing.reshape(shape)).reshape(outgoing.shape)
    produced = run_expert(arrived, w_gate[0], w_up[0], w_down[0])
    returned = everywhere(produced.reshape(shape)).reshape(outgoing.shape)
    parcels = combine(returned, rank, gate, spot)
    landed = everywhere(parcels.reshape(experts, 8, parcels.shape[3])).reshape(experts * 8, parcels.shape[3])
    keep, give = join(landed, stream)

    mine = jnp.stack([keep, to_partner(give)])
    blocks = [along(mine, hops) for hops in range(4)]
    near, far = turning_tables(tokens, 16)
    kv, norm = project_keys(blocks, attn_gain.reshape(1, -1), k_gain.reshape(KVH, HD), w_key, w_value, near, far)
    all_kv = lax.all_to_all(
        jnp.broadcast_to(kv[None], (16, *kv.shape)), "ctx", split_axis=0, concat_axis=0, tiled=True
    )
    low, high = project_queries(norm, to_partner(norm), w_query, q_gain, near, far)
    for_partner = attend(to_partner(low), to_partner(high), all_kv)
    from_partner = to_partner(for_partner)
    folded = attend(low, high, all_kv)
    attended, sent = merge_and_project(folded, from_partner, w_out)
    received = to_partner(sent)
    kept = project_own(attended, w_out)
    total = mine.astype(F32)
    for hops in range(4):
        pair = (kept[hops].astype(F32) + received[hops].astype(F32)).astype(BF16)
        total = total + along(pair, hops).astype(F32)
    total = total.astype(BF16)
    other = to_partner(total[1])
    return jnp.where(core == 0, jnp.concatenate([total[0], other], 0), jnp.concatenate([other, total[0]], 0))


def solution(mesh):
    in_specs = (
        P(("ctx", "head"), None),
        P(("ctx", "head"), None),
        P(("ctx", "head")),
        P(),
        P(("ctx", "head"), None, None),
        P(("ctx", "head"), None, None),
        P(("ctx", "head"), None, None),
        P("ctx", "head"),
        P(),
        P("head"),
        P(),
        P(None, "head"),
        P(),
        P(),
        P("head", None),
    )
    out_specs = P("ctx", "head")
    return jax.shard_map(body, mesh=mesh, in_specs=in_specs, out_specs=out_specs, check_vma=False)
```

```python
import math

import jax
import jax.numpy as jnp
import numpy as np
from jax import lax
from jax.experimental import pallas as pl
from jax.experimental.pallas import tpu as pltpu
from jax.sharding import PartitionSpec as P

QH = 32
KVH = 4
HD = 128
EPSILON = 1e-06
THETA = 1000000.0
F32 = jnp.float32
BF16 = jnp.bfloat16
VMEM = pltpu.VMEM
NEG = -1e30
MIB = 1024 * 1024


def iota(shape, dim):
    return lax.broadcasted_iota(jnp.int32, shape, dim)


def dot(a, b):
    return jnp.dot(a, b, preferred_element_type=F32)


def dot_t(a, b):
    return lax.dot_general(a, b, (((1,), (1,)), ((), ())), preferred_element_type=F32)


def start_loads(pairs, sems):
    loads = [pltpu.make_async_copy(source, target, sems.at[i]) for i, (source, target) in enumerate(pairs)]
    for load in loads:
        load.start()
    return loads


def dispatch_kernel(
    rows_hbm, ids_hbm, targets_hbm, router_hbm, y_hbm, rank_ref, gate_ref, spot_ref,
    y_ref, rows_ref, ids_ref, targets_ref, router_ref, sems,
):
    loads = start_loads(
        [(targets_hbm, targets_ref), (ids_hbm, ids_ref), (rows_hbm, rows_ref), (router_hbm, router_ref)], sems
    )
    n, width = rows_ref.shape
    for load in loads[:3]:
        load.wait()
    experts = router_ref.shape[1]
    first = iota((n, n), 0)
    second = iota((n, n), 1)
    owner = jnp.broadcast_to((targets_ref[...] // 512).astype(F32), (n, n))
    same = jnp.where((owner.T == owner) & (first < second), 1.0, 0.0)
    place = owner[0:1] * 8.0 + jnp.sum(same, 0, keepdims=True)
    perm = jnp.where(first.astype(F32) == place, 1.0, 0.0)
    spot = (targets_ref[...] % 512).astype(F32)
    spot_ref[...] = jnp.broadcast_to(jnp.sum(perm * spot, 1, keepdims=True), (n, 128))
    perm = perm.astype(BF16)
    rows = dot(perm, rows_ref[...]).astype(BF16)
    ids = dot_t(ids_ref[...].astype(F32).astype(BF16), perm)
    expert = iota((experts, n), 0).astype(F32)
    member = jnp.zeros((experts, n), F32)
    for k in range(ids.shape[0]):
        member = member + jnp.where(expert == ids[k : k + 1, :], 1.0, 0.0)
    before = jnp.where(first < second, 1.0, 0.0).astype(BF16)
    rank = jnp.where(member > 0.5, dot(member.astype(BF16), before), -1.0)
    half = width // 2
    blk = 32
    packed = rank.astype(BF16)
    stores = []
    for i in range(experts // blk):
        spread = jnp.where(iota((blk * 8, experts), 0) // 8 + i * blk == iota((blk * 8, experts), 1), 1.0, 0.0)
        rank_e = dot(spread.astype(BF16), packed)
        slot = (iota(rank_e.shape, 0) % 8).astype(F32)
        main = jnp.where(rank_e == slot, 1.0, 0.0).astype(BF16)
        low = jnp.where((rank_e == slot + 8.0) & (slot < 4.0), 1.0, 0.0).astype(BF16)
        high = jnp.where((rank_e == slot + 4.0) & (slot >= 4.0), 1.0, 0.0).astype(BF16)
        lines = slice(i * blk * 8, (i + 1) * blk * 8)
        y_ref[lines, :width] = dot(main, rows).astype(BF16)
        y_ref[lines, width:] = (dot(low, rows[:, :half]) + dot(high, rows[:, half:])).astype(BF16)
        stores.append(pltpu.make_async_copy(y_ref.at[lines], y_hbm.at[lines], sems.at[4 + i]))
        stores[-1].start()
    rank_ref[...] = rank.T
    member_q = member.T > 0.5
    loads[3].wait()
    logits = dot(rows, router_ref[...])
    highest = jnp.max(jnp.where(member_q, logits, NEG), 1, keepdims=True)
    raised = jnp.where(member_q, jnp.exp(jnp.minimum(logits - highest, 0.0)), 0.0)
    gate_ref[...] = raised / jnp.sum(raised, 1, keepdims=True)
    for store in stores:
        store.wait()


def dispatch(rows, ids, targets, router):
    n, width = rows.shape
    table = jax.ShapeDtypeStruct((n, 128), F32)
    return pl.pallas_call(
        dispatch_kernel,
        in_specs=[pl.BlockSpec(memory_space=pltpu.HBM)] * 4,
        out_specs=[pl.BlockSpec(memory_space=pltpu.HBM)] + [pl.BlockSpec(memory_space=VMEM)] * 3,
        out_shape=[jax.ShapeDtypeStruct((1024, width * 3 // 2), BF16), table, table, table],
        scratch_shapes=[
            VMEM((1024, width * 3 // 2), BF16),
            VMEM((n, width), BF16),
            VMEM((8, n), jnp.int32),
            VMEM((1, n), jnp.int32),
            VMEM(router.shape, BF16),
            pltpu.SemaphoreType.DMA((8,)),
        ],
        compiler_params=pltpu.CompilerParams(vmem_limit_bytes=57 * MIB),
        name="dispatch_rows",
    )(rows, ids.T, targets.reshape(1, n), router)


def expert_kernel(y_ref, wg_ref, wu_ref, wd_ref, o_ref):
    rows = 256
    half_rows = rows // 2
    width = wg_ref.shape[0]
    half = width // 2
    r = iota((half_rows, rows), 0)
    col = iota((half_rows, rows), 1)
    source = r // 4 * 8 + r % 4
    low = jnp.where(col == source, 1.0, 0.0).astype(BF16)
    high = jnp.where(col == source + 4, 1.0, 0.0).astype(BF16)
    rt = iota((rows, half_rows), 0)
    ct = iota((rows, half_rows), 1)
    target = ct // 4 * 8 + ct % 4
    low_t = jnp.where(rt == target, 1.0, 0.0).astype(BF16)
    high_t = jnp.where(rt == target + 4, 1.0, 0.0).astype(BF16)
    for i in range(y_ref.shape[0] // rows):
        lines = slice(i * rows, (i + 1) * rows)
        extra = y_ref[lines, width:]
        inputs = jnp.concatenate(
            [
                y_ref[lines, :width],
                jnp.concatenate([dot(low, extra).astype(BF16), dot(high, extra).astype(BF16)], 1),
            ],
            0,
        )
        gate_part = dot(inputs, wg_ref[...])
        upward = dot(inputs, wu_ref[...])
        hidden = (gate_part / (1.0 + jnp.exp(-gate_part)) * upward).astype(BF16)
        produced = dot(hidden, wd_ref[...]).astype(BF16)
        o_ref[lines, :width] = produced[:rows]
        o_ref[lines, width:] = (dot(low_t, produced[rows:, :half]) + dot(high_t, produced[rows:, half:])).astype(BF16)


def run_expert(y, w_gate, w_up, w_down):
    return pl.pallas_call(
        expert_kernel,
        out_shape=jax.ShapeDtypeStruct(y.shape, BF16),
        compiler_params=pltpu.CompilerParams(vmem_limit_bytes=16 * MIB),
        name="expert_ffn",
    )(y, w_gate, w_up, w_down)


def combine_kernel(r_ref, rank_ref, gate_ref, spot_ref, o_ref):
    n, experts = rank_ref.shape
    rows = r_ref.shape[0]
    width = r_ref.shape[1] * 2 // 3
    spread = jnp.where(iota((experts, rows), 0) == iota((experts, rows), 1) // 8, 1.0, 0.0).astype(BF16)
    gate = gate_ref[...]
    gate_hi = gate.astype(BF16)
    gate_lo = (gate - gate_hi.astype(F32)).astype(BF16)
    rank_e = dot(rank_ref[...].astype(BF16), spread)
    slot = (iota(rank_e.shape, 1) % 8).astype(F32)
    gates = [dot(gate_hi, spread), dot(gate_lo, spread)]

    def chosen(mask):
        return jnp.concatenate([jnp.where(mask, g, 0.0).astype(BF16) for g in gates], 0)

    main = chosen(rank_e == slot)
    extras = [chosen((rank_e == slot + 8.0) & (slot < 4.0)), chosen((rank_e == slot + 4.0) & (slot >= 4.0))]
    spot = spot_ref[...]
    lane = iota(spot.shape, 1)
    big = jnp.floor(spot * (1.0 / 16.0))
    tail = jnp.where(lane == 0, big, jnp.where(lane == 1, spot - 16.0 * big, 0.0))
    tail = tail.reshape(n // 8, 8, 128).astype(BF16)
    parts = o_ref.shape[1]
    w = width // parts
    span = width // 4
    for c in range(4):
        lines = slice(c * span, (c + 1) * span)
        more = width + (c % 2) * span
        merged = dot(main, r_ref[:, lines]) + dot(extras[c // 2], r_ref[:, more : more + span])
        merged = merged[:n] + merged[n:]
        for i in range(span // w):
            o_ref[:, c * (span // w) + i, :, :w] = merged[:, i * w : (i + 1) * w].reshape(n // 8, 8, w).astype(BF16)
    for h in range(parts):
        o_ref[:, h, :, w:] = tail


def combine(r, rank, gate, spot):
    n = rank.shape[0]
    width = r.shape[1] * 2 // 3
    return pl.pallas_call(
        combine_kernel,
        out_shape=jax.ShapeDtypeStruct((n // 8, 8, 8, width // 8 + 128), BF16),
        compiler_params=pltpu.CompilerParams(vmem_limit_bytes=16 * MIB),
        name="combine_rows",
    )(r, rank, gate, spot)


def join_kernel(landed_ref, stream_ref, keep_ref, give_ref):
    core = lax.rem(lax.axis_index("head"), 2)
    tokens, w = stream_ref.shape
    half = tokens // 2
    tail = landed_ref[:, w:].astype(F32)
    spot = tail[:, 0:1] * 16.0 + tail[:, 1:2]
    count = landed_ref.shape[0]
    hit = jnp.where(spot == iota((count, tokens), 1).astype(F32), 1.0, 0.0).astype(BF16)
    added = lax.dot_general(hit, landed_ref[:, :w], (((0,), (0,)), ((), ())), preferred_element_type=F32)
    joined = stream_ref[...].astype(F32) + added
    keep_ref[...] = jnp.where(core == 0, joined[:half], joined[half:]).astype(BF16)
    give_ref[...] = jnp.where(core == 0, joined[half:], joined[:half]).astype(BF16)


def join(landed, stream):
    part = jax.ShapeDtypeStruct((stream.shape[0] // 2, stream.shape[1]), BF16)
    return pl.pallas_call(
        join_kernel,
        out_shape=[part, part],
        compiler_params=pltpu.CompilerParams(vmem_limit_bytes=16 * MIB),
        name="join_rows",
    )(landed, stream)


def turning_tables(tokens, shards):
    frequency = THETA ** (-np.arange(HD // 2, dtype=np.float64) * 2.0 / HD)

    def table(positions):
        angles = np.asarray(positions, np.float64)[:, None] * np.concatenate([frequency, frequency])[None, :]
        return np.stack([np.cos(angles), np.sin(angles)]).astype(np.float32)

    return table(np.arange(tokens)), table(np.arange(shards) * tokens)


def turned(vectors, gains, near, far, shard):
    mean = jnp.mean(vectors * vectors, -1, keepdims=True)
    vectors = vectors * lax.rsqrt(mean + EPSILON) * gains
    far_cos = far[0][pl.ds(shard, 1), :]
    far_sin = far[1][pl.ds(shard, 1), :]
    cos = near[0] * far_cos - near[1] * far_sin
    sin = near[1] * far_cos + near[0] * far_sin
    sign = jnp.where(iota((1, HD), 1) < HD // 2, -1.0, 1.0)
    return vectors * cos + pltpu.roll(vectors, HD // 2, 1) * (sin * sign)


def keys_kernel(x0, x1, x2, x3, gain_ref, kg_ref, wk_hbm, wv_hbm, near_ref, far_ref, kv_hbm, norm_hbm, kv_ref, norm_ref, wkv_ref, sems):
    ctx = lax.axis_index("ctx")
    head = lax.axis_index("head")
    z = head // 2
    core = lax.rem(head, 2)
    x_refs = (x0, x1, x2, x3)
    columns = pl.ds(pl.multiple_of(z * HD, HD), HD)
    loads = start_loads(
        [(wk_hbm.at[:, columns], wkv_ref.at[:, :HD]), (wv_hbm.at[:, columns], wkv_ref.at[:, HD:])], sems
    )
    _, half, w = x0.shape
    width = 8 * w
    square = jnp.zeros((half, 1), F32)
    for x_ref in x_refs:
        for j in range(2):
            x = x_ref[j].astype(F32)
            square = square + jnp.sum(x * x, 1, keepdims=True)
    scale = lax.rsqrt(square * (1.0 / width) + EPSILON)
    for i, x_ref in enumerate(x_refs):
        for j in range(2):
            block = 2 * lax.rem(z + 4 - i, 4) + (core if j == 0 else 1 - core)
            norm = (x_ref[j].astype(F32) * scale * gain_ref[:, pl.ds(pl.multiple_of(block * w, w), w)]).astype(BF16)
            norm_ref[:, pl.ds(pl.multiple_of(block * w, w), w)] = norm
    stores = [pltpu.make_async_copy(norm_ref, norm_hbm, sems.at[2])]
    stores[0].start()
    for load in loads:
        load.wait()
    both = dot(norm_ref[...], wkv_ref[...])
    shard = jnp.where(core == 0, ctx, far_ref.shape[1] - 1 - ctx)
    near = [jnp.where(core == 0, near_ref[t, :half], near_ref[t, half:]) for t in range(2)]
    far = [far_ref.at[0], far_ref.at[1]]
    kv_ref[:, :HD] = turned(both[:, :HD], kg_ref[pl.ds(z, 1), :], near, far, shard).astype(BF16)
    kv_ref[:, HD:] = both[:, HD:].astype(BF16)
    for i in range(kv_hbm.shape[0]):
        stores.append(pltpu.make_async_copy(kv_ref, kv_hbm.at[i], sems.at[3 + i]))
        stores[-1].start()
    for store in stores:
        store.wait()


def project_keys(blocks, row_gain, key_gain, w_key, w_value, near, far):
    _, half, w = blocks[0].shape
    return pl.pallas_call(
        keys_kernel,
        in_specs=[pl.BlockSpec(memory_space=VMEM)] * 6
        + [pl.BlockSpec(memory_space=pltpu.HBM)] * 2
        + [pl.BlockSpec(memory_space=VMEM)] * 2,
        out_specs=[pl.BlockSpec(memory_space=pltpu.HBM)] * 2,
        out_shape=[
            jax.ShapeDtypeStruct((far.shape[1], half, 2 * HD), BF16),
            jax.ShapeDtypeStruct((half, 8 * w), BF16),
        ],
        scratch_shapes=[
            VMEM((half, 2 * HD), BF16),
            VMEM((half, 8 * w), BF16),
            VMEM((w_key.shape[0], 2 * HD), BF16),
            pltpu.SemaphoreType.DMA((3 + far.shape[1],)),
        ],
        compiler_params=pltpu.CompilerParams(vmem_limit_bytes=16 * MIB),
        name="project_keys",
    )(*blocks, row_gain, key_gain, w_key, w_value, near, far)


def queries_kernel(own_ref, other_ref, wq_ref, qg_ref, near_ref, far_ref, low_ref, high_ref):
    ctx = lax.axis_index("ctx")
    core = lax.rem(lax.axis_index("head"), 2)
    half = own_ref.shape[0]
    factor = math.log2(math.e) / math.sqrt(HD)
    far = [far_ref.at[0], far_ref.at[1]]
    for upper, o_ref in enumerate((low_ref, high_ref)):
        norm = jnp.where(core == upper, own_ref[...], other_ref[...])
        queries = dot(norm, wq_ref[...])
        shard = ctx if upper == 0 else far_ref.shape[1] - 1 - ctx
        near = [near_ref[t, upper * half : (upper + 1) * half] for t in range(2)]
        for h in range(o_ref.shape[0]):
            part = slice(h * HD, (h + 1) * HD)
            o_ref[h] = (turned(queries[:, part], qg_ref[:, part], near, far, shard) * factor).astype(BF16)


def project_queries(own, other, w_query, q_gain, near, far):
    heads = w_query.shape[1] // HD
    part = jax.ShapeDtypeStruct((heads, own.shape[0], HD), BF16)
    return pl.pallas_call(
        queries_kernel,
        out_shape=[part, part],
        compiler_params=pltpu.CompilerParams(vmem_limit_bytes=16 * MIB),
        name="project_queries",
    )(own, other, w_query, q_gain.reshape(1, -1), near, far)


def attend_kernel(low_ref, high_ref, kv_ref, o_ref, value_s):
    ctx = lax.axis_index("ctx")
    core = lax.rem(lax.axis_index("head"), 2)
    shards, shard, _ = kv_ref.shape
    heads, half, _ = low_ref.shape
    group = 4
    subs = 2
    span = group * shard
    rows = heads * half // subs
    value_s[:, :, :HD] = kv_ref[:, :, HD:]
    value_s[:, :, HD:] = jnp.ones((shards, shard, HD), BF16)

    for upper, q_ref in enumerate((low_ref, high_ref)):
        own = ctx if upper == 0 else shards - 1 - ctx
        queries = q_ref[...].reshape(heads * half, HD)
        pieces = [queries[i * rows : (i + 1) * rows] for i in range(subs)]

        def fold(carry, chunk, masked):
            first = jnp.where(core == 0, chunk, shards // group - 1 - chunk) * group
            keys = kv_ref[pl.ds(first, group), :, :HD].reshape(span, HD)
            values = value_s[pl.ds(first, group)].reshape(span, 2 * HD)
            if masked:
                t = iota((1, span), 1)
                place = first + t // shard
                key_pos = jnp.where(core == 0, place, shards - 1 - place) * (2 * shard) + core * shard + t % shard
                query_pos = own * (2 * half) + upper * half + iota((half, span), 0)
                bias = jnp.where(query_pos >= key_pos, 0.0, NEG)
            every = [dot_t(piece, keys) for piece in pieces]
            result = []
            for (highest, weighted), scores in zip(carry, every):
                if masked:
                    scores = (scores.reshape(rows // half, half, span) + bias[None]).reshape(rows, span)
                fresh = jnp.maximum(highest, jnp.max(scores, 1, keepdims=True))
                weights = jnp.exp2(scores - fresh)
                weighted = weighted * jnp.exp2(highest - fresh) + dot(weights.astype(BF16), values)
                result.append((fresh, weighted))
            return tuple(result)

        start = tuple((jnp.full((rows, 1), 0.5 * NEG, F32), jnp.zeros((rows, 2 * HD), F32)) for _ in range(subs))
        whole = own // group
        state = lax.fori_loop(0, whole, lambda j, carry: fold(carry, j, False), start)
        state = fold(state, whole, True)
        lane = iota((rows, HD), 1)
        for i, (highest, weighted) in enumerate(state):
            part = slice(i * (heads // subs), (i + 1) * (heads // subs))
            o_ref[part, upper * half : (upper + 1) * half, :HD] = weighted[:, :HD].reshape(heads // subs, half, HD)
            stats = jnp.where(lane < HD // 2, highest, weighted[:, HD:])
            o_ref[part, upper * half : (upper + 1) * half, HD:] = stats.reshape(heads // subs, half, HD)


def attend(low, high, kv):
    heads, half, _ = low.shape
    return pl.pallas_call(
        attend_kernel,
        out_shape=jax.ShapeDtypeStruct((heads, 2 * half, 2 * HD), F32),
        scratch_shapes=[VMEM(kv.shape, BF16)],
        compiler_params=pltpu.CompilerParams(vmem_limit_bytes=28 * MIB),
        name="attend",
    )(low, high, kv)


def project_blocks(attended, core, w_ref, o_ref):
    z = lax.axis_index("head") // 2
    w = o_ref.shape[3]
    for i in range(o_ref.shape[0]):
        for j in range(2):
            block = 2 * lax.rem(z + i, 4) + (core if j == 0 else 1 - core)
            o_ref[i, j] = dot(attended, w_ref[:, pl.ds(pl.multiple_of(block * w, w), w)]).astype(BF16)


def merge_kernel(own_ref, other_ref, w_ref, keep_ref, o_ref):
    core = lax.rem(lax.axis_index("head"), 2)
    half = keep_ref.shape[0]
    given = []
    for h in range(own_ref.shape[0]):
        m0 = own_ref[h, :, HD : HD + 1]
        m1 = other_ref[h, :, HD : HD + 1]
        top = jnp.maximum(m0, m1)
        e0 = jnp.exp2(m0 - top)
        e1 = jnp.exp2(m1 - top)
        total = own_ref[h, :, 2 * HD - 1 :] * e0 + other_ref[h, :, 2 * HD - 1 :] * e1
        share = 1.0 / total
        value = own_ref[h, :, :HD] * (e0 * share) + other_ref[h, :, :HD] * (e1 * share)
        keep_ref[:, h * HD : (h + 1) * HD] = jnp.where(core == 0, value[:half], value[half:]).astype(BF16)
        given.append(jnp.where(core == 0, value[half:], value[:half]).astype(BF16))
    project_blocks(jnp.concatenate(given, 1), 1 - core, w_ref, o_ref)


def own_kernel(attended_ref, w_ref, o_ref):
    project_blocks(attended_ref[...], lax.rem(lax.axis_index("head"), 2), w_ref, o_ref)


def merge_and_project(own, other, w_out):
    heads, tokens, _ = own.shape
    return pl.pallas_call(
        merge_kernel,
        out_shape=[
            jax.ShapeDtypeStruct((tokens // 2, heads * HD), BF16),
            jax.ShapeDtypeStruct((4, 2, tokens // 2, w_out.shape[1] // 8), BF16),
        ],
        compiler_params=pltpu.CompilerParams(vmem_limit_bytes=16 * MIB),
        name="merge_and_project",
    )(own, other, w_out)


def project_own(attended, w_out):
    return pl.pallas_call(
        own_kernel,
        out_shape=jax.ShapeDtypeStruct((4, 2, attended.shape[0], w_out.shape[1] // 8), BF16),
        compiler_params=pltpu.CompilerParams(vmem_limit_bytes=16 * MIB),
        name="project_own",
    )(attended, w_out)


def body(
    branch_rows,
    expert_ids,
    targets,
    router,
    w_gate,
    w_up,
    w_down,
    stream,
    attn_gain,
    q_gain,
    k_gain,
    w_query,
    w_key,
    w_value,
    w_out,
):
    core = lax.axis_index("head") % 2
    experts = router.shape[1]
    tokens, w = stream.shape
    partner = [(i, i ^ 1) for i in range(8)]

    def to_partner(shard):
        return lax.ppermute(shard, "head", partner)

    def along(shard, hops):
        pairs = []
        for c in range(16):
            for h in range(8):
                there = c if h % 2 == 0 else 15 - c
                pairs.append((c * 8 + h, there * 8 + (h + 2 * hops) % 8))
        return lax.ppermute(shard, ("ctx", "head"), pairs)

    def everywhere(blocks):
        return lax.all_to_all(blocks, ("ctx", "head"), split_axis=0, concat_axis=0, tiled=True)

    outgoing, rank, gate, spot = dispatch(branch_rows, expert_ids, targets, router)
    shape = (experts, 8, outgoing.shape[1])
    arrived = everywhere(outgoing.reshape(shape)).reshape(outgoing.shape)
    produced = run_expert(arrived, w_gate[0], w_up[0], w_down[0])
    returned = everywhere(produced.reshape(shape)).reshape(outgoing.shape)
    parcels = combine(returned, rank, gate, spot)
    landed = everywhere(parcels.reshape(experts, 8, parcels.shape[3])).reshape(experts * 8, parcels.shape[3])
    keep, give = join(landed, stream)

    mine = jnp.stack([keep, to_partner(give)])
    blocks = [along(mine, hops) for hops in range(4)]
    near, far = turning_tables(tokens, 16)
    kv, norm = project_keys(blocks, attn_gain.reshape(1, -1), k_gain.reshape(KVH, HD), w_key, w_value, near, far)
    all_kv = lax.all_to_all(kv, "ctx", split_axis=0, concat_axis=0, tiled=True)
    low, high = project_queries(norm, to_partner(norm), w_query, q_gain, near, far)
    for_partner = attend(to_partner(low), to_partner(high), all_kv)
    from_partner = to_partner(for_partner)
    folded = attend(low, high, all_kv)
    attended, sent = merge_and_project(folded, from_partner, w_out)
    received = to_partner(sent)
    kept = project_own(attended, w_out)
    total = mine.astype(F32)
    for hops in range(4):
        pair = (kept[hops].astype(F32) + received[hops].astype(F32)).astype(BF16)
        total = total + along(pair, hops).astype(F32)
    total = total.astype(BF16)
    other = to_partner(total[1])
    return jnp.where(core == 0, jnp.concatenate([total[0], other], 0), jnp.concatenate([other, total[0]], 0))


def solution(mesh):
    in_specs = (
        P(("ctx", "head"), None),
        P(("ctx", "head"), None),
        P(("ctx", "head")),
        P(),
        P(("ctx", "head"), None, None),
        P(("ctx", "head"), None, None),
        P(("ctx", "head"), None, None),
        P("ctx", "head"),
        P(),
        P("head"),
        P(),
        P(None, "head"),
        P(),
        P(),
        P("head", None),
    )
    out_specs = P("ctx", "head")
    return jax.shard_map(body, mesh=mesh, in_specs=in_specs, out_specs=out_specs, check_vma=False)
```

```python
import math

import jax
import jax.numpy as jnp
import numpy as np
from jax import lax
from jax.experimental import pallas as pl
from jax.experimental.pallas import tpu as pltpu
from jax.sharding import PartitionSpec as P

QH = 32
KVH = 4
HD = 128
EPSILON = 1e-06
THETA = 1000000.0
F32 = jnp.float32
BF16 = jnp.bfloat16
VMEM = pltpu.VMEM
NEG = -1e30
MIB = 1024 * 1024


def iota(shape, dim):
    return lax.broadcasted_iota(jnp.int32, shape, dim)


def dot(a, b):
    return jnp.dot(a, b, preferred_element_type=F32)


def dot_t(a, b):
    return lax.dot_general(a, b, (((1,), (1,)), ((), ())), preferred_element_type=F32)


def start_loads(pairs, sems):
    loads = [pltpu.make_async_copy(source, target, sems.at[i]) for i, (source, target) in enumerate(pairs)]
    for load in loads:
        load.start()
    return loads


def dispatch_kernel(
    rows_hbm, ids_hbm, targets_hbm, router_hbm, y_hbm, rank_ref, gate_ref, spot_ref,
    y_ref, rows_ref, ids_ref, targets_ref, router_ref, sems,
):
    loads = start_loads(
        [(targets_hbm, targets_ref), (ids_hbm, ids_ref), (rows_hbm, rows_ref), (router_hbm, router_ref)], sems
    )
    n, width = rows_ref.shape
    for load in loads[:3]:
        load.wait()
    experts = router_ref.shape[1]
    first = iota((n, n), 0)
    second = iota((n, n), 1)
    owner = jnp.broadcast_to((targets_ref[...] // 512).astype(F32), (n, n))
    same = jnp.where((owner.T == owner) & (first < second), 1.0, 0.0)
    place = owner[0:1] * 8.0 + jnp.sum(same, 0, keepdims=True)
    perm = jnp.where(first.astype(F32) == place, 1.0, 0.0)
    spot = (targets_ref[...] % 512).astype(F32)
    spot_ref[...] = jnp.broadcast_to(jnp.sum(perm * spot, 1, keepdims=True), (n, 128))
    perm = perm.astype(BF16)
    rows = dot(perm, rows_ref[...]).astype(BF16)
    ids = dot_t(ids_ref[...].astype(F32).astype(BF16), perm)
    expert = iota((experts, n), 0).astype(F32)
    member = jnp.zeros((experts, n), F32)
    for k in range(ids.shape[0]):
        member = member + jnp.where(expert == ids[k : k + 1, :], 1.0, 0.0)
    before = jnp.where(first < second, 1.0, 0.0).astype(BF16)
    rank = jnp.where(member > 0.5, dot(member.astype(BF16), before), -1.0)
    half = width // 2
    blk = 32
    packed = rank.astype(BF16)
    stores = []
    for i in range(experts // blk):
        spread = jnp.where(iota((blk * 8, experts), 0) // 8 + i * blk == iota((blk * 8, experts), 1), 1.0, 0.0)
        rank_e = dot(spread.astype(BF16), packed)
        slot = (iota(rank_e.shape, 0) % 8).astype(F32)
        main = jnp.where(rank_e == slot, 1.0, 0.0).astype(BF16)
        low = jnp.where((rank_e == slot + 8.0) & (slot < 4.0), 1.0, 0.0).astype(BF16)
        high = jnp.where((rank_e == slot + 4.0) & (slot >= 4.0), 1.0, 0.0).astype(BF16)
        lines = slice(i * blk * 8, (i + 1) * blk * 8)
        y_ref[lines, :width] = dot(main, rows).astype(BF16)
        y_ref[lines, width:] = (dot(low, rows[:, :half]) + dot(high, rows[:, half:])).astype(BF16)
        stores.append(pltpu.make_async_copy(y_ref.at[lines], y_hbm.at[lines], sems.at[4 + i]))
        stores[-1].start()
    rank_ref[...] = rank.T
    member_q = member.T > 0.5
    loads[3].wait()
    logits = dot(rows, router_ref[...])
    highest = jnp.max(jnp.where(member_q, logits, NEG), 1, keepdims=True)
    raised = jnp.where(member_q, jnp.exp(jnp.minimum(logits - highest, 0.0)), 0.0)
    gate_ref[...] = raised / jnp.sum(raised, 1, keepdims=True)
    for store in stores:
        store.wait()


def dispatch(rows, ids, targets, router):
    n, width = rows.shape
    table = jax.ShapeDtypeStruct((n, 128), F32)
    return pl.pallas_call(
        dispatch_kernel,
        in_specs=[pl.BlockSpec(memory_space=pltpu.HBM)] * 4,
        out_specs=[pl.BlockSpec(memory_space=pltpu.HBM)] + [pl.BlockSpec(memory_space=VMEM)] * 3,
        out_shape=[jax.ShapeDtypeStruct((1024, width * 3 // 2), BF16), table, table, table],
        scratch_shapes=[
            VMEM((1024, width * 3 // 2), BF16),
            VMEM((n, width), BF16),
            VMEM((8, n), jnp.int32),
            VMEM((1, n), jnp.int32),
            VMEM(router.shape, BF16),
            pltpu.SemaphoreType.DMA((8,)),
        ],
        compiler_params=pltpu.CompilerParams(vmem_limit_bytes=57 * MIB),
        name="dispatch_rows",
    )(rows, ids.T, targets.reshape(1, n), router)


def expert_kernel(y_ref, wg_ref, wu_ref, wd_ref, o_ref):
    rows = 256
    half_rows = rows // 2
    width = wg_ref.shape[0]
    half = width // 2
    r = iota((half_rows, rows), 0)
    col = iota((half_rows, rows), 1)
    source = r // 4 * 8 + r % 4
    low = jnp.where(col == source, 1.0, 0.0).astype(BF16)
    high = jnp.where(col == source + 4, 1.0, 0.0).astype(BF16)
    rt = iota((rows, half_rows), 0)
    ct = iota((rows, half_rows), 1)
    target = ct // 4 * 8 + ct % 4
    low_t = jnp.where(rt == target, 1.0, 0.0).astype(BF16)
    high_t = jnp.where(rt == target + 4, 1.0, 0.0).astype(BF16)
    for i in range(y_ref.shape[0] // rows):
        lines = slice(i * rows, (i + 1) * rows)
        extra = y_ref[lines, width:]
        inputs = jnp.concatenate(
            [
                y_ref[lines, :width],
                jnp.concatenate([dot(low, extra).astype(BF16), dot(high, extra).astype(BF16)], 1),
            ],
            0,
        )
        gate_part = dot(inputs, wg_ref[...])
        upward = dot(inputs, wu_ref[...])
        hidden = (gate_part / (1.0 + jnp.exp(-gate_part)) * upward).astype(BF16)
        produced = dot(hidden, wd_ref[...]).astype(BF16)
        o_ref[lines, :width] = produced[:rows]
        o_ref[lines, width:] = (dot(low_t, produced[rows:, :half]) + dot(high_t, produced[rows:, half:])).astype(BF16)


def run_expert(y, w_gate, w_up, w_down):
    return pl.pallas_call(
        expert_kernel,
        out_shape=jax.ShapeDtypeStruct(y.shape, BF16),
        compiler_params=pltpu.CompilerParams(vmem_limit_bytes=16 * MIB),
        name="expert_ffn",
    )(y, w_gate, w_up, w_down)


def combine_kernel(r_ref, rank_ref, gate_ref, spot_ref, o_ref):
    n, experts = rank_ref.shape
    rows = r_ref.shape[0]
    width = r_ref.shape[1] * 2 // 3
    spread = jnp.where(iota((experts, rows), 0) == iota((experts, rows), 1) // 8, 1.0, 0.0).astype(BF16)
    gate = gate_ref[...]
    gate_hi = gate.astype(BF16)
    gate_lo = (gate - gate_hi.astype(F32)).astype(BF16)
    rank_e = dot(rank_ref[...].astype(BF16), spread)
    slot = (iota(rank_e.shape, 1) % 8).astype(F32)
    gates = [dot(gate_hi, spread), dot(gate_lo, spread)]

    def chosen(mask):
        return jnp.concatenate([jnp.where(mask, g, 0.0).astype(BF16) for g in gates], 0)

    main = chosen(rank_e == slot)
    extras = [chosen((rank_e == slot + 8.0) & (slot < 4.0)), chosen((rank_e == slot + 4.0) & (slot >= 4.0))]
    spot = spot_ref[...]
    lane = iota(spot.shape, 1)
    big = jnp.floor(spot * (1.0 / 16.0))
    tail = jnp.where(lane == 0, big, jnp.where(lane == 1, spot - 16.0 * big, 0.0))
    tail = tail.reshape(n // 8, 8, 128).astype(BF16)
    parts = o_ref.shape[1]
    w = width // parts
    span = width // 4
    for c in range(4):
        lines = slice(c * span, (c + 1) * span)
        more = width + (c % 2) * span
        merged = dot(main, r_ref[:, lines]) + dot(extras[c // 2], r_ref[:, more : more + span])
        merged = merged[:n] + merged[n:]
        for i in range(span // w):
            o_ref[:, c * (span // w) + i, :, :w] = merged[:, i * w : (i + 1) * w].reshape(n // 8, 8, w).astype(BF16)
    for h in range(parts):
        o_ref[:, h, :, w:] = tail


def combine(r, rank, gate, spot):
    n = rank.shape[0]
    width = r.shape[1] * 2 // 3
    return pl.pallas_call(
        combine_kernel,
        out_shape=jax.ShapeDtypeStruct((n // 8, 8, 8, width // 8 + 128), BF16),
        compiler_params=pltpu.CompilerParams(vmem_limit_bytes=16 * MIB),
        name="combine_rows",
    )(r, rank, gate, spot)


def join_kernel(landed_ref, stream_ref, keep_ref, give_ref):
    core = lax.rem(lax.axis_index("head"), 2)
    tokens, w = stream_ref.shape
    half = tokens // 2
    tail = landed_ref[:, w:].astype(F32)
    spot = tail[:, 0:1] * 16.0 + tail[:, 1:2]
    count = landed_ref.shape[0]
    hit = jnp.where(spot == iota((count, tokens), 1).astype(F32), 1.0, 0.0).astype(BF16)
    added = lax.dot_general(hit, landed_ref[:, :w], (((0,), (0,)), ((), ())), preferred_element_type=F32)
    joined = stream_ref[...].astype(F32) + added
    keep_ref[...] = jnp.where(core == 0, joined[:half], joined[half:]).astype(BF16)
    give_ref[...] = jnp.where(core == 0, joined[half:], joined[:half]).astype(BF16)


def join(landed, stream):
    part = jax.ShapeDtypeStruct((stream.shape[0] // 2, stream.shape[1]), BF16)
    return pl.pallas_call(
        join_kernel,
        out_shape=[part, part],
        compiler_params=pltpu.CompilerParams(vmem_limit_bytes=16 * MIB),
        name="join_rows",
    )(landed, stream)


def turning_tables(tokens, shards):
    frequency = THETA ** (-np.arange(HD // 2, dtype=np.float64) * 2.0 / HD)

    def table(positions):
        angles = np.asarray(positions, np.float64)[:, None] * np.concatenate([frequency, frequency])[None, :]
        return np.stack([np.cos(angles), np.sin(angles)]).astype(np.float32)

    return table(np.arange(tokens)), table(np.arange(shards) * tokens)


def turned(vectors, gains, near, far, shard):
    mean = jnp.mean(vectors * vectors, -1, keepdims=True)
    vectors = vectors * lax.rsqrt(mean + EPSILON) * gains
    far_cos = far[0][pl.ds(shard, 1), :]
    far_sin = far[1][pl.ds(shard, 1), :]
    cos = near[0] * far_cos - near[1] * far_sin
    sin = near[1] * far_cos + near[0] * far_sin
    sign = jnp.where(iota((1, HD), 1) < HD // 2, -1.0, 1.0)
    return vectors * cos + pltpu.roll(vectors, HD // 2, 1) * (sin * sign)


def keys_kernel(x0, x1, x2, x3, gain_ref, kg_ref, wk_hbm, wv_hbm, near_ref, far_ref, kv_ref, norm_ref, wkv_ref, sems):
    ctx = lax.axis_index("ctx")
    head = lax.axis_index("head")
    z = head // 2
    core = lax.rem(head, 2)
    x_refs = (x0, x1, x2, x3)
    columns = pl.ds(pl.multiple_of(z * HD, HD), HD)
    loads = start_loads(
        [(wk_hbm.at[:, columns], wkv_ref.at[:, :HD]), (wv_hbm.at[:, columns], wkv_ref.at[:, HD:])], sems
    )
    _, half, w = x0.shape
    width = 8 * w
    square = jnp.zeros((half, 1), F32)
    for x_ref in x_refs:
        for j in range(2):
            x = x_ref[j].astype(F32)
            square = square + jnp.sum(x * x, 1, keepdims=True)
    scale = lax.rsqrt(square * (1.0 / width) + EPSILON)
    for i, x_ref in enumerate(x_refs):
        source = lax.rem(jnp.where(core == 0, z + 4 - i, z + i), 4)
        for j in range(2):
            block = 2 * source + (core if j == 0 else 1 - core)
            norm = (x_ref[j].astype(F32) * scale * gain_ref[:, pl.ds(pl.multiple_of(block * w, w), w)]).astype(BF16)
            norm_ref[:, pl.ds(pl.multiple_of(block * w, w), w)] = norm
    for load in loads:
        load.wait()
    both = dot(norm_ref[...], wkv_ref[...])
    shard = jnp.where(core == 0, ctx, far_ref.shape[1] - 1 - ctx)
    near = [jnp.where(core == 0, near_ref[t, :half], near_ref[t, half:]) for t in range(2)]
    far = [far_ref.at[0], far_ref.at[1]]
    kv_ref[:, :HD] = turned(both[:, :HD], kg_ref[pl.ds(z, 1), :], near, far, shard).astype(BF16)
    kv_ref[:, HD:] = both[:, HD:].astype(BF16)


def project_keys(blocks, row_gain, key_gain, w_key, w_value, near, far):
    _, half, w = blocks[0].shape
    return pl.pallas_call(
        keys_kernel,
        in_specs=[pl.BlockSpec(memory_space=VMEM)] * 6
        + [pl.BlockSpec(memory_space=pltpu.HBM)] * 2
        + [pl.BlockSpec(memory_space=VMEM)] * 2,
        out_shape=[jax.ShapeDtypeStruct((half, 2 * HD), BF16), jax.ShapeDtypeStruct((half, 8 * w), BF16)],
        scratch_shapes=[VMEM((w_key.shape[0], 2 * HD), BF16), pltpu.SemaphoreType.DMA((2,))],
        compiler_params=pltpu.CompilerParams(vmem_limit_bytes=16 * MIB),
        name="project_keys",
    )(*blocks, row_gain, key_gain, w_key, w_value, near, far)


def queries_kernel(own_ref, other_ref, wq_ref, qg_ref, near_ref, far_ref, low_ref, high_ref):
    ctx = lax.axis_index("ctx")
    core = lax.rem(lax.axis_index("head"), 2)
    half = own_ref.shape[0]
    factor = math.log2(math.e) / math.sqrt(HD)
    far = [far_ref.at[0], far_ref.at[1]]
    for upper, o_ref in enumerate((low_ref, high_ref)):
        norm = jnp.where(core == upper, own_ref[...], other_ref[...])
        queries = dot(norm, wq_ref[...])
        shard = ctx if upper == 0 else far_ref.shape[1] - 1 - ctx
        near = [near_ref[t, upper * half : (upper + 1) * half] for t in range(2)]
        for h in range(o_ref.shape[0]):
            part = slice(h * HD, (h + 1) * HD)
            o_ref[h] = (turned(queries[:, part], qg_ref[:, part], near, far, shard) * factor).astype(BF16)


def project_queries(own, other, w_query, q_gain, near, far):
    heads = w_query.shape[1] // HD
    part = jax.ShapeDtypeStruct((heads, own.shape[0], HD), BF16)
    return pl.pallas_call(
        queries_kernel,
        out_shape=[part, part],
        compiler_params=pltpu.CompilerParams(vmem_limit_bytes=16 * MIB),
        name="project_queries",
    )(own, other, w_query, q_gain.reshape(1, -1), near, far)


def attend_kernel(low_ref, high_ref, kv_ref, o_ref, value_s):
    ctx = lax.axis_index("ctx")
    core = lax.rem(lax.axis_index("head"), 2)
    shards, shard, _ = kv_ref.shape
    heads, half, _ = low_ref.shape
    group = 4
    subs = 2
    span = group * shard
    rows = heads * half // subs
    value_s[:, :, :HD] = kv_ref[:, :, HD:]
    value_s[:, :, HD:] = jnp.ones((shards, shard, HD), BF16)

    for upper, q_ref in enumerate((low_ref, high_ref)):
        own = ctx if upper == 0 else shards - 1 - ctx
        queries = q_ref[...].reshape(heads * half, HD)
        pieces = [queries[i * rows : (i + 1) * rows] for i in range(subs)]

        def fold(carry, chunk, masked):
            first = jnp.where(core == 0, chunk, shards // group - 1 - chunk) * group
            keys = kv_ref[pl.ds(first, group), :, :HD].reshape(span, HD)
            values = value_s[pl.ds(first, group)].reshape(span, 2 * HD)
            if masked:
                t = iota((1, span), 1)
                place = first + t // shard
                key_pos = jnp.where(core == 0, place, shards - 1 - place) * (2 * shard) + core * shard + t % shard
                query_pos = own * (2 * half) + upper * half + iota((half, span), 0)
                bias = jnp.where(query_pos >= key_pos, 0.0, NEG)
            every = [dot_t(piece, keys) for piece in pieces]
            result = []
            for (highest, weighted), scores in zip(carry, every):
                if masked:
                    scores = (scores.reshape(rows // half, half, span) + bias[None]).reshape(rows, span)
                fresh = jnp.maximum(highest, jnp.max(scores, 1, keepdims=True))
                weights = jnp.exp2(scores - fresh)
                weighted = weighted * jnp.exp2(highest - fresh) + dot(weights.astype(BF16), values)
                result.append((fresh, weighted))
            return tuple(result)

        start = tuple((jnp.full((rows, 1), 0.5 * NEG, F32), jnp.zeros((rows, 2 * HD), F32)) for _ in range(subs))
        whole = own // group
        state = lax.fori_loop(0, whole, lambda j, carry: fold(carry, j, False), start)
        state = fold(state, whole, True)
        lane = iota((rows, HD), 1)
        for i, (highest, weighted) in enumerate(state):
            part = slice(i * (heads // subs), (i + 1) * (heads // subs))
            o_ref[part, upper * half : (upper + 1) * half, :HD] = weighted[:, :HD].reshape(heads // subs, half, HD)
            stats = jnp.where(lane < HD // 2, highest, weighted[:, HD:])
            o_ref[part, upper * half : (upper + 1) * half, HD:] = stats.reshape(heads // subs, half, HD)


def attend(low, high, kv):
    heads, half, _ = low.shape
    return pl.pallas_call(
        attend_kernel,
        out_shape=jax.ShapeDtypeStruct((heads, 2 * half, 2 * HD), F32),
        scratch_shapes=[VMEM(kv.shape, BF16)],
        compiler_params=pltpu.CompilerParams(vmem_limit_bytes=28 * MIB),
        name="attend",
    )(low, high, kv)


def project_blocks(attended, core, w_ref, o_ref):
    z = lax.axis_index("head") // 2
    w = o_ref.shape[3]
    for i in range(o_ref.shape[0]):
        target = lax.rem(jnp.where(core == 0, z + i, z + 4 - i), 4)
        for j in range(2):
            block = 2 * target + (core if j == 0 else 1 - core)
            o_ref[i, j] = dot(attended, w_ref[:, pl.ds(pl.multiple_of(block * w, w), w)]).astype(BF16)


def merge_kernel(own_ref, other_ref, w_ref, keep_ref, o_ref):
    core = lax.rem(lax.axis_index("head"), 2)
    half = keep_ref.shape[0]
    given = []
    for h in range(own_ref.shape[0]):
        m0 = own_ref[h, :, HD : HD + 1]
        m1 = other_ref[h, :, HD : HD + 1]
        top = jnp.maximum(m0, m1)
        e0 = jnp.exp2(m0 - top)
        e1 = jnp.exp2(m1 - top)
        total = own_ref[h, :, 2 * HD - 1 :] * e0 + other_ref[h, :, 2 * HD - 1 :] * e1
        share = 1.0 / total
        value = own_ref[h, :, :HD] * (e0 * share) + other_ref[h, :, :HD] * (e1 * share)
        keep_ref[:, h * HD : (h + 1) * HD] = jnp.where(core == 0, value[:half], value[half:]).astype(BF16)
        given.append(jnp.where(core == 0, value[half:], value[:half]).astype(BF16))
    project_blocks(jnp.concatenate(given, 1), 1 - core, w_ref, o_ref)


def own_kernel(attended_ref, w_ref, o_ref):
    project_blocks(attended_ref[...], lax.rem(lax.axis_index("head"), 2), w_ref, o_ref)


def merge_and_project(own, other, w_out):
    heads, tokens, _ = own.shape
    return pl.pallas_call(
        merge_kernel,
        out_shape=[
            jax.ShapeDtypeStruct((tokens // 2, heads * HD), BF16),
            jax.ShapeDtypeStruct((4, 2, tokens // 2, w_out.shape[1] // 8), BF16),
        ],
        compiler_params=pltpu.CompilerParams(vmem_limit_bytes=16 * MIB),
        name="merge_and_project",
    )(own, other, w_out)


def project_own(attended, w_out):
    return pl.pallas_call(
        own_kernel,
        out_shape=jax.ShapeDtypeStruct((4, 2, attended.shape[0], w_out.shape[1] // 8), BF16),
        compiler_params=pltpu.CompilerParams(vmem_limit_bytes=16 * MIB),
        name="project_own",
    )(attended, w_out)


def body(
    branch_rows,
    expert_ids,
    targets,
    router,
    w_gate,
    w_up,
    w_down,
    stream,
    attn_gain,
    q_gain,
    k_gain,
    w_query,
    w_key,
    w_value,
    w_out,
):
    core = lax.axis_index("head") % 2
    experts = router.shape[1]
    tokens, w = stream.shape
    partner = [(i, i ^ 1) for i in range(8)]

    def to_partner(shard):
        return lax.ppermute(shard, "head", partner)

    def along(shard, hops):
        pairs = []
        for c in range(16):
            for h in range(8):
                there = c * 8 + (h + 2 * hops) % 8 if h % 2 == 0 else (15 - c) * 8 + (h - 2 * hops) % 8
                pairs.append((c * 8 + h, there))
        return lax.ppermute(shard, ("ctx", "head"), pairs)

    def everywhere(blocks):
        return lax.all_to_all(blocks, ("ctx", "head"), split_axis=0, concat_axis=0, tiled=True)

    outgoing, rank, gate, spot = dispatch(branch_rows, expert_ids, targets, router)
    shape = (experts, 8, outgoing.shape[1])
    arrived = everywhere(outgoing.reshape(shape)).reshape(outgoing.shape)
    produced = run_expert(arrived, w_gate[0], w_up[0], w_down[0])
    returned = everywhere(produced.reshape(shape)).reshape(outgoing.shape)
    parcels = combine(returned, rank, gate, spot)
    landed = everywhere(parcels.reshape(experts, 8, parcels.shape[3])).reshape(experts * 8, parcels.shape[3])
    keep, give = join(landed, stream)

    mine = jnp.stack([keep, to_partner(give)])
    blocks = [along(mine, hops) for hops in range(4)]
    near, far = turning_tables(tokens, 16)
    kv, norm = project_keys(blocks, attn_gain.reshape(1, -1), k_gain.reshape(KVH, HD), w_key, w_value, near, far)
    all_kv = lax.all_to_all(
        jnp.broadcast_to(kv[None], (16, *kv.shape)), "ctx", split_axis=0, concat_axis=0, tiled=True
    )
    low, high = project_queries(norm, to_partner(norm), w_query, q_gain, near, far)
    for_partner = attend(to_partner(low), to_partner(high), all_kv)
    from_partner = to_partner(for_partner)
    folded = attend(low, high, all_kv)
    attended, sent = merge_and_project(folded, from_partner, w_out)
    received = to_partner(sent)
    kept = project_own(attended, w_out)
    total = mine.astype(F32)
    for hops in range(4):
        pair = (kept[hops].astype(F32) + received[hops].astype(F32)).astype(BF16)
        total = total + along(pair, hops).astype(F32)
    total = total.astype(BF16)
    other = to_partner(total[1])
    return jnp.where(core == 0, jnp.concatenate([total[0], other], 0), jnp.concatenate([other, total[0]], 0))


def solution(mesh):
    in_specs = (
        P(("ctx", "head"), None),
        P(("ctx", "head"), None),
        P(("ctx", "head")),
        P(),
        P(("ctx", "head"), None, None),
        P(("ctx", "head"), None, None),
        P(("ctx", "head"), None, None),
        P("ctx", "head"),
        P(),
        P("head"),
        P(),
        P(None, "head"),
        P(),
        P(),
        P("head", None),
    )
    out_specs = P("ctx", "head")
    return jax.shard_map(body, mesh=mesh, in_specs=in_specs, out_specs=out_specs, check_vma=False)
```

```python
import math

import jax
import jax.numpy as jnp
import numpy as np
from jax import lax
from jax.experimental import pallas as pl
from jax.experimental.pallas import tpu as pltpu
from jax.sharding import PartitionSpec as P

QH = 32
KVH = 4
HD = 128
EPSILON = 1e-06
THETA = 1000000.0
F32 = jnp.float32
BF16 = jnp.bfloat16
VMEM = pltpu.VMEM
NEG = -1e30
MIB = 1024 * 1024
GROUP = 4


def iota(shape, dim):
    return lax.broadcasted_iota(jnp.int32, shape, dim)


def dot(a, b):
    return jnp.dot(a, b, preferred_element_type=F32)


def dot_t(a, b):
    return lax.dot_general(a, b, (((1,), (1,)), ((), ())), preferred_element_type=F32)


def start_loads(pairs, sems):
    loads = [pltpu.make_async_copy(source, target, sems.at[i]) for i, (source, target) in enumerate(pairs)]
    for load in loads:
        load.start()
    return loads


def dispatch_kernel(
    rows_hbm, ids_hbm, targets_hbm, router_hbm, y_hbm, rank_ref, gate_ref, spot_ref,
    y_ref, rows_ref, ids_ref, targets_ref, router_ref, sems,
):
    loads = start_loads(
        [(targets_hbm, targets_ref), (ids_hbm, ids_ref), (rows_hbm, rows_ref), (router_hbm, router_ref)], sems
    )
    n, width = rows_ref.shape
    for load in loads[:3]:
        load.wait()
    experts = router_ref.shape[1]
    first = iota((n, n), 0)
    second = iota((n, n), 1)
    owner = jnp.broadcast_to((targets_ref[...] // 512).astype(F32), (n, n))
    same = jnp.where((owner.T == owner) & (first < second), 1.0, 0.0)
    place = owner[0:1] * 8.0 + jnp.sum(same, 0, keepdims=True)
    perm = jnp.where(first.astype(F32) == place, 1.0, 0.0)
    spot = (targets_ref[...] % 512).astype(F32)
    spot_ref[...] = jnp.broadcast_to(jnp.sum(perm * spot, 1, keepdims=True), (n, 128))
    perm = perm.astype(BF16)
    rows = dot(perm, rows_ref[...]).astype(BF16)
    ids = dot_t(ids_ref[...].astype(F32).astype(BF16), perm)
    expert = iota((experts, n), 0).astype(F32)
    member = jnp.zeros((experts, n), F32)
    for k in range(ids.shape[0]):
        member = member + jnp.where(expert == ids[k : k + 1, :], 1.0, 0.0)
    before = jnp.where(first < second, 1.0, 0.0).astype(BF16)
    rank = jnp.where(member > 0.5, dot(member.astype(BF16), before), -1.0)
    half = width // 2
    blk = 32
    packed = rank.astype(BF16)
    stores = []
    for i in range(experts // blk):
        spread = jnp.where(iota((blk * 8, experts), 0) // 8 + i * blk == iota((blk * 8, experts), 1), 1.0, 0.0)
        rank_e = dot(spread.astype(BF16), packed)
        slot = (iota(rank_e.shape, 0) % 8).astype(F32)
        main = jnp.where(rank_e == slot, 1.0, 0.0).astype(BF16)
        low = jnp.where((rank_e == slot + 8.0) & (slot < 4.0), 1.0, 0.0).astype(BF16)
        high = jnp.where((rank_e == slot + 4.0) & (slot >= 4.0), 1.0, 0.0).astype(BF16)
        lines = slice(i * blk * 8, (i + 1) * blk * 8)
        y_ref[lines, :width] = dot(main, rows).astype(BF16)
        y_ref[lines, width:] = (dot(low, rows[:, :half]) + dot(high, rows[:, half:])).astype(BF16)
        stores.append(pltpu.make_async_copy(y_ref.at[lines], y_hbm.at[lines], sems.at[4 + i]))
        stores[-1].start()
    rank_ref[...] = rank.T
    member_q = member.T > 0.5
    loads[3].wait()
    logits = dot(rows, router_ref[...])
    highest = jnp.max(jnp.where(member_q, logits, NEG), 1, keepdims=True)
    raised = jnp.where(member_q, jnp.exp(jnp.minimum(logits - highest, 0.0)), 0.0)
    gate_ref[...] = raised / jnp.sum(raised, 1, keepdims=True)
    for store in stores:
        store.wait()


def dispatch(rows, ids, targets, router):
    n, width = rows.shape
    table = jax.ShapeDtypeStruct((n, 128), F32)
    return pl.pallas_call(
        dispatch_kernel,
        in_specs=[pl.BlockSpec(memory_space=pltpu.HBM)] * 4,
        out_specs=[pl.BlockSpec(memory_space=pltpu.HBM)] + [pl.BlockSpec(memory_space=VMEM)] * 3,
        out_shape=[jax.ShapeDtypeStruct((1024, width * 3 // 2), BF16), table, table, table],
        scratch_shapes=[
            VMEM((1024, width * 3 // 2), BF16),
            VMEM((n, width), BF16),
            VMEM((8, n), jnp.int32),
            VMEM((1, n), jnp.int32),
            VMEM(router.shape, BF16),
            pltpu.SemaphoreType.DMA((8,)),
        ],
        compiler_params=pltpu.CompilerParams(vmem_limit_bytes=57 * MIB),
        name="dispatch_rows",
    )(rows, ids.T, targets.reshape(1, n), router)


def expert_kernel(y_ref, wg_ref, wu_ref, wd_ref, o_ref):
    rows = 256
    half_rows = rows // 2
    width = wg_ref.shape[0]
    half = width // 2
    r = iota((half_rows, rows), 0)
    col = iota((half_rows, rows), 1)
    source = r // 4 * 8 + r % 4
    low = jnp.where(col == source, 1.0, 0.0).astype(BF16)
    high = jnp.where(col == source + 4, 1.0, 0.0).astype(BF16)
    rt = iota((rows, half_rows), 0)
    ct = iota((rows, half_rows), 1)
    target = ct // 4 * 8 + ct % 4
    low_t = jnp.where(rt == target, 1.0, 0.0).astype(BF16)
    high_t = jnp.where(rt == target + 4, 1.0, 0.0).astype(BF16)
    for i in range(y_ref.shape[0] // rows):
        lines = slice(i * rows, (i + 1) * rows)
        extra = y_ref[lines, width:]
        inputs = jnp.concatenate(
            [
                y_ref[lines, :width],
                jnp.concatenate([dot(low, extra).astype(BF16), dot(high, extra).astype(BF16)], 1),
            ],
            0,
        )
        gate_part = dot(inputs, wg_ref[...])
        upward = dot(inputs, wu_ref[...])
        hidden = (gate_part / (1.0 + jnp.exp(-gate_part)) * upward).astype(BF16)
        produced = dot(hidden, wd_ref[...]).astype(BF16)
        o_ref[lines, :width] = produced[:rows]
        o_ref[lines, width:] = (dot(low_t, produced[rows:, :half]) + dot(high_t, produced[rows:, half:])).astype(BF16)


def run_expert(y, w_gate, w_up, w_down):
    return pl.pallas_call(
        expert_kernel,
        out_shape=jax.ShapeDtypeStruct(y.shape, BF16),
        compiler_params=pltpu.CompilerParams(vmem_limit_bytes=16 * MIB),
        name="expert_ffn",
    )(y, w_gate, w_up, w_down)


def combine_kernel(r_ref, rank_ref, gate_ref, spot_ref, o_ref):
    n, experts = rank_ref.shape
    rows = r_ref.shape[0]
    width = r_ref.shape[1] * 2 // 3
    spread = jnp.where(iota((experts, rows), 0) == iota((experts, rows), 1) // 8, 1.0, 0.0).astype(BF16)
    gate = gate_ref[...]
    gate_hi = gate.astype(BF16)
    gate_lo = (gate - gate_hi.astype(F32)).astype(BF16)
    rank_e = dot(rank_ref[...].astype(BF16), spread)
    slot = (iota(rank_e.shape, 1) % 8).astype(F32)
    gates = [dot(gate_hi, spread), dot(gate_lo, spread)]

    def chosen(mask):
        return jnp.concatenate([jnp.where(mask, g, 0.0).astype(BF16) for g in gates], 0)

    main = chosen(rank_e == slot)
    extras = [chosen((rank_e == slot + 8.0) & (slot < 4.0)), chosen((rank_e == slot + 4.0) & (slot >= 4.0))]
    spot = spot_ref[...]
    lane = iota(spot.shape, 1)
    big = jnp.floor(spot * (1.0 / 16.0))
    tail = jnp.where(lane == 0, big, jnp.where(lane == 1, spot - 16.0 * big, 0.0))
    tail = tail.reshape(n // 8, 8, 128).astype(BF16)
    parts = o_ref.shape[1]
    w = width // parts
    span = width // 4
    for c in range(4):
        lines = slice(c * span, (c + 1) * span)
        more = width + (c % 2) * span
        merged = dot(main, r_ref[:, lines]) + dot(extras[c // 2], r_ref[:, more : more + span])
        merged = merged[:n] + merged[n:]
        for i in range(span // w):
            o_ref[:, c * (span // w) + i, :, :w] = merged[:, i * w : (i + 1) * w].reshape(n // 8, 8, w).astype(BF16)
    for h in range(parts):
        o_ref[:, h, :, w:] = tail


def combine(r, rank, gate, spot):
    n = rank.shape[0]
    width = r.shape[1] * 2 // 3
    return pl.pallas_call(
        combine_kernel,
        out_shape=jax.ShapeDtypeStruct((n // 8, 8, 8, width // 8 + 128), BF16),
        compiler_params=pltpu.CompilerParams(vmem_limit_bytes=16 * MIB),
        name="combine_rows",
    )(r, rank, gate, spot)


def join_kernel(landed_ref, stream_ref, keep_ref, give_ref):
    core = lax.rem(lax.axis_index("head"), 2)
    tokens, w = stream_ref.shape
    half = tokens // 2
    tail = landed_ref[:, w:].astype(F32)
    spot = tail[:, 0:1] * 16.0 + tail[:, 1:2]
    count = landed_ref.shape[0]
    hit = jnp.where(spot == iota((count, tokens), 1).astype(F32), 1.0, 0.0).astype(BF16)
    added = lax.dot_general(hit, landed_ref[:, :w], (((0,), (0,)), ((), ())), preferred_element_type=F32)
    joined = stream_ref[...].astype(F32) + added
    keep_ref[...] = jnp.where(core == 0, joined[:half], joined[half:]).astype(BF16)
    give_ref[...] = jnp.where(core == 0, joined[half:], joined[:half]).astype(BF16)


def join(landed, stream):
    part = jax.ShapeDtypeStruct((stream.shape[0] // 2, stream.shape[1]), BF16)
    return pl.pallas_call(
        join_kernel,
        out_shape=[part, part],
        compiler_params=pltpu.CompilerParams(vmem_limit_bytes=16 * MIB),
        name="join_rows",
    )(landed, stream)


def mirrored(shard):
    return shard + 16 - GROUP - 2 * GROUP * (shard // GROUP)


def turning_tables(tokens, shards):
    frequency = THETA ** (-np.arange(HD // 2, dtype=np.float64) * 2.0 / HD)

    def table(positions):
        angles = np.asarray(positions, np.float64)[:, None] * np.concatenate([frequency, frequency])[None, :]
        return np.stack([np.cos(angles), np.sin(angles)]).astype(np.float32)

    return table(np.arange(tokens)), table(np.arange(shards) * tokens)


def turned(vectors, gains, near, far, shard):
    mean = jnp.mean(vectors * vectors, -1, keepdims=True)
    vectors = vectors * lax.rsqrt(mean + EPSILON) * gains
    far_cos = far[0][pl.ds(shard, 1), :]
    far_sin = far[1][pl.ds(shard, 1), :]
    cos = near[0] * far_cos - near[1] * far_sin
    sin = near[1] * far_cos + near[0] * far_sin
    sign = jnp.where(iota((1, HD), 1) < HD // 2, -1.0, 1.0)
    return vectors * cos + pltpu.roll(vectors, HD // 2, 1) * (sin * sign)


def keys_kernel(x0, x1, x2, x3, gain_ref, kg_ref, wk_hbm, wv_hbm, near_ref, far_ref, kv_ref, norm_ref, wkv_ref, sems):
    ctx = lax.axis_index("ctx")
    head = lax.axis_index("head")
    z = head // 2
    core = lax.rem(head, 2)
    x_refs = (x0, x1, x2, x3)
    columns = pl.ds(pl.multiple_of(z * HD, HD), HD)
    loads = start_loads(
        [(wk_hbm.at[:, columns], wkv_ref.at[:, :HD]), (wv_hbm.at[:, columns], wkv_ref.at[:, HD:])], sems
    )
    _, half, w = x0.shape
    width = 8 * w
    square = jnp.zeros((half, 1), F32)
    for x_ref in x_refs:
        for j in range(2):
            x = x_ref[j].astype(F32)
            square = square + jnp.sum(x * x, 1, keepdims=True)
    scale = lax.rsqrt(square * (1.0 / width) + EPSILON)
    for i, x_ref in enumerate(x_refs):
        source = lax.rem(z + 4 - i, 4)
        for j in range(2):
            block = 2 * source + (core if j == 0 else 1 - core)
            norm = (x_ref[j].astype(F32) * scale * gain_ref[:, pl.ds(pl.multiple_of(block * w, w), w)]).astype(BF16)
            norm_ref[:, pl.ds(pl.multiple_of(block * w, w), w)] = norm
    for load in loads:
        load.wait()
    both = dot(norm_ref[...], wkv_ref[...])
    shard = jnp.where(core == 0, ctx, mirrored(ctx))
    near = [jnp.where(core == 0, near_ref[t, :half], near_ref[t, half:]) for t in range(2)]
    far = [far_ref.at[0], far_ref.at[1]]
    kv_ref[:, :HD] = turned(both[:, :HD], kg_ref[pl.ds(z, 1), :], near, far, shard).astype(BF16)
    kv_ref[:, HD:] = both[:, HD:].astype(BF16)


def project_keys(blocks, row_gain, key_gain, w_key, w_value, near, far):
    _, half, w = blocks[0].shape
    return pl.pallas_call(
        keys_kernel,
        in_specs=[pl.BlockSpec(memory_space=VMEM)] * 6
        + [pl.BlockSpec(memory_space=pltpu.HBM)] * 2
        + [pl.BlockSpec(memory_space=VMEM)] * 2,
        out_shape=[jax.ShapeDtypeStruct((half, 2 * HD), BF16), jax.ShapeDtypeStruct((half, 8 * w), BF16)],
        scratch_shapes=[VMEM((w_key.shape[0], 2 * HD), BF16), pltpu.SemaphoreType.DMA((2,))],
        compiler_params=pltpu.CompilerParams(vmem_limit_bytes=16 * MIB),
        name="project_keys",
    )(*blocks, row_gain, key_gain, w_key, w_value, near, far)


def queries_kernel(own_ref, other_ref, wq_ref, qg_ref, near_ref, far_ref, low_ref, high_ref):
    ctx = lax.axis_index("ctx")
    core = lax.rem(lax.axis_index("head"), 2)
    half = own_ref.shape[0]
    factor = math.log2(math.e) / math.sqrt(HD)
    far = [far_ref.at[0], far_ref.at[1]]
    for upper, o_ref in enumerate((low_ref, high_ref)):
        norm = jnp.where(core == upper, own_ref[...], other_ref[...])
        queries = dot(norm, wq_ref[...])
        shard = ctx if upper == 0 else mirrored(ctx)
        near = [near_ref[t, upper * half : (upper + 1) * half] for t in range(2)]
        for h in range(o_ref.shape[0]):
            part = slice(h * HD, (h + 1) * HD)
            o_ref[h] = (turned(queries[:, part], qg_ref[:, part], near, far, shard) * factor).astype(BF16)


def project_queries(own, other, w_query, q_gain, near, far):
    heads = w_query.shape[1] // HD
    part = jax.ShapeDtypeStruct((heads, own.shape[0], HD), BF16)
    return pl.pallas_call(
        queries_kernel,
        out_shape=[part, part],
        compiler_params=pltpu.CompilerParams(vmem_limit_bytes=16 * MIB),
        name="project_queries",
    )(own, other, w_query, q_gain.reshape(1, -1), near, far)


def attend_kernel(low_ref, high_ref, kv_ref, o_ref, value_s):
    ctx = lax.axis_index("ctx")
    core = lax.rem(lax.axis_index("head"), 2)
    shards, shard, _ = kv_ref.shape
    heads, half, _ = low_ref.shape
    group = GROUP
    subs = 2
    span = group * shard
    rows = heads * half // subs
    value_s[:, :, :HD] = kv_ref[:, :, HD:]
    value_s[:, :, HD:] = jnp.ones((shards, shard, HD), BF16)

    for upper, q_ref in enumerate((low_ref, high_ref)):
        own = ctx if upper == 0 else mirrored(ctx)
        queries = q_ref[...].reshape(heads * half, HD)
        pieces = [queries[i * rows : (i + 1) * rows] for i in range(subs)]

        def fold(carry, chunk, masked):
            first = jnp.where(core == 0, chunk, shards // group - 1 - chunk) * group
            keys = kv_ref[pl.ds(first, group), :, :HD].reshape(span, HD)
            values = value_s[pl.ds(first, group)].reshape(span, 2 * HD)
            if masked:
                t = iota((1, span), 1)
                key_pos = (chunk * group + t // shard) * (2 * shard) + core * shard + t % shard
                query_pos = own * (2 * half) + upper * half + iota((half, span), 0)
                bias = jnp.where(query_pos >= key_pos, 0.0, NEG)
            every = [dot_t(piece, keys) for piece in pieces]
            result = []
            for (highest, weighted), scores in zip(carry, every):
                if masked:
                    scores = (scores.reshape(rows // half, half, span) + bias[None]).reshape(rows, span)
                fresh = jnp.maximum(highest, jnp.max(scores, 1, keepdims=True))
                weights = jnp.exp2(scores - fresh)
                weighted = weighted * jnp.exp2(highest - fresh) + dot(weights.astype(BF16), values)
                result.append((fresh, weighted))
            return tuple(result)

        start = tuple((jnp.full((rows, 1), 0.5 * NEG, F32), jnp.zeros((rows, 2 * HD), F32)) for _ in range(subs))
        whole = own // group
        state = lax.fori_loop(0, whole, lambda j, carry: fold(carry, j, False), start)
        state = fold(state, whole, True)
        lane = iota((rows, HD), 1)
        for i, (highest, weighted) in enumerate(state):
            part = slice(i * (heads // subs), (i + 1) * (heads // subs))
            o_ref[part, upper * half : (upper + 1) * half, :HD] = weighted[:, :HD].reshape(heads // subs, half, HD)
            stats = jnp.where(lane < HD // 2, highest, weighted[:, HD:])
            o_ref[part, upper * half : (upper + 1) * half, HD:] = stats.reshape(heads // subs, half, HD)


def attend(low, high, kv):
    heads, half, _ = low.shape
    return pl.pallas_call(
        attend_kernel,
        out_shape=jax.ShapeDtypeStruct((heads, 2 * half, 2 * HD), F32),
        scratch_shapes=[VMEM(kv.shape, BF16)],
        compiler_params=pltpu.CompilerParams(vmem_limit_bytes=28 * MIB),
        name="attend",
    )(low, high, kv)


def project_blocks(attended, core, w_ref, o_ref):
    z = lax.axis_index("head") // 2
    w = o_ref.shape[3]
    for i in range(o_ref.shape[0]):
        target = lax.rem(z + i, 4)
        for j in range(2):
            block = 2 * target + (core if j == 0 else 1 - core)
            o_ref[i, j] = dot(attended, w_ref[:, pl.ds(pl.multiple_of(block * w, w), w)]).astype(BF16)


def merge_kernel(own_ref, other_ref, w_ref, keep_ref, o_ref):
    core = lax.rem(lax.axis_index("head"), 2)
    half = keep_ref.shape[0]
    given = []
    for h in range(own_ref.shape[0]):
        m0 = own_ref[h, :, HD : HD + 1]
        m1 = other_ref[h, :, HD : HD + 1]
        top = jnp.maximum(m0, m1)
        e0 = jnp.exp2(m0 - top)
        e1 = jnp.exp2(m1 - top)
        total = own_ref[h, :, 2 * HD - 1 :] * e0 + other_ref[h, :, 2 * HD - 1 :] * e1
        share = 1.0 / total
        value = own_ref[h, :, :HD] * (e0 * share) + other_ref[h, :, :HD] * (e1 * share)
        keep_ref[:, h * HD : (h + 1) * HD] = jnp.where(core == 0, value[:half], value[half:]).astype(BF16)
        given.append(jnp.where(core == 0, value[half:], value[:half]).astype(BF16))
    project_blocks(jnp.concatenate(given, 1), 1 - core, w_ref, o_ref)


def own_kernel(attended_ref, w_ref, o_ref):
    project_blocks(attended_ref[...], lax.rem(lax.axis_index("head"), 2), w_ref, o_ref)


def merge_and_project(own, other, w_out):
    heads, tokens, _ = own.shape
    return pl.pallas_call(
        merge_kernel,
        out_shape=[
            jax.ShapeDtypeStruct((tokens // 2, heads * HD), BF16),
            jax.ShapeDtypeStruct((4, 2, tokens // 2, w_out.shape[1] // 8), BF16),
        ],
        compiler_params=pltpu.CompilerParams(vmem_limit_bytes=16 * MIB),
        name="merge_and_project",
    )(own, other, w_out)


def project_own(attended, w_out):
    return pl.pallas_call(
        own_kernel,
        out_shape=jax.ShapeDtypeStruct((4, 2, attended.shape[0], w_out.shape[1] // 8), BF16),
        compiler_params=pltpu.CompilerParams(vmem_limit_bytes=16 * MIB),
        name="project_own",
    )(attended, w_out)


def body(
    branch_rows,
    expert_ids,
    targets,
    router,
    w_gate,
    w_up,
    w_down,
    stream,
    attn_gain,
    q_gain,
    k_gain,
    w_query,
    w_key,
    w_value,
    w_out,
):
    core = lax.axis_index("head") % 2
    experts = router.shape[1]
    tokens, w = stream.shape
    partner = [(i, i ^ 1) for i in range(8)]

    def to_partner(shard):
        return lax.ppermute(shard, "head", partner)

    def along(shard, hops):
        pairs = []
        for c in range(16):
            for h in range(8):
                there = c if h % 2 == 0 else mirrored(c)
                pairs.append((c * 8 + h, there * 8 + (h + 2 * hops) % 8))
        return lax.ppermute(shard, ("ctx", "head"), pairs)

    def everywhere(blocks):
        return lax.all_to_all(blocks, ("ctx", "head"), split_axis=0, concat_axis=0, tiled=True)

    outgoing, rank, gate, spot = dispatch(branch_rows, expert_ids, targets, router)
    shape = (experts, 8, outgoing.shape[1])
    arrived = everywhere(outgoing.reshape(shape)).reshape(outgoing.shape)
    produced = run_expert(arrived, w_gate[0], w_up[0], w_down[0])
    returned = everywhere(produced.reshape(shape)).reshape(outgoing.shape)
    parcels = combine(returned, rank, gate, spot)
    landed = everywhere(parcels.reshape(experts, 8, parcels.shape[3])).reshape(experts * 8, parcels.shape[3])
    keep, give = join(landed, stream)

    mine = jnp.stack([keep, to_partner(give)])
    blocks = [along(mine, hops) for hops in range(4)]
    near, far = turning_tables(tokens, 16)
    kv, norm = project_keys(blocks, attn_gain.reshape(1, -1), k_gain.reshape(KVH, HD), w_key, w_value, near, far)
    all_kv = lax.all_to_all(
        jnp.broadcast_to(kv[None], (16, *kv.shape)), "ctx", split_axis=0, concat_axis=0, tiled=True
    )
    low, high = project_queries(norm, to_partner(norm), w_query, q_gain, near, far)
    for_partner = attend(to_partner(low), to_partner(high), all_kv)
    from_partner = to_partner(for_partner)
    folded = attend(low, high, all_kv)
    attended, sent = merge_and_project(folded, from_partner, w_out)
    received = to_partner(sent)
    kept = project_own(attended, w_out)
    total = mine.astype(F32)
    for hops in range(4):
        pair = (kept[hops].astype(F32) + received[hops].astype(F32)).astype(BF16)
        total = total + along(pair, hops).astype(F32)
    total = total.astype(BF16)
    other = to_partner(total[1])
    return jnp.where(core == 0, jnp.concatenate([total[0], other], 0), jnp.concatenate([other, total[0]], 0))


def solution(mesh):
    in_specs = (
        P(("ctx", "head"), None),
        P(("ctx", "head"), None),
        P(("ctx", "head")),
        P(),
        P(("ctx", "head"), None, None),
        P(("ctx", "head"), None, None),
        P(("ctx", "head"), None, None),
        P("ctx", "head"),
        P(),
        P("head"),
        P(),
        P(None, "head"),
        P(),
        P(),
        P("head", None),
    )
    out_specs = P("ctx", "head")
    return jax.shard_map(body, mesh=mesh, in_specs=in_specs, out_specs=out_specs, check_vma=False)
```

```python
import math

import jax
import jax.numpy as jnp
import numpy as np
from jax import lax
from jax.experimental import pallas as pl
from jax.experimental.pallas import tpu as pltpu
from jax.sharding import PartitionSpec as P

QH = 32
KVH = 4
HD = 128
EPSILON = 1e-06
THETA = 1000000.0
F32 = jnp.float32
BF16 = jnp.bfloat16
VMEM = pltpu.VMEM
NEG = -1e30
MIB = 1024 * 1024


def iota(shape, dim):
    return lax.broadcasted_iota(jnp.int32, shape, dim)


def dot(a, b):
    return jnp.dot(a, b, preferred_element_type=F32)


def dot_t(a, b):
    return lax.dot_general(a, b, (((1,), (1,)), ((), ())), preferred_element_type=F32)


def start_loads(pairs, sems):
    loads = [pltpu.make_async_copy(source, target, sems.at[i]) for i, (source, target) in enumerate(pairs)]
    for load in loads:
        load.start()
    return loads


def dispatch_kernel(
    rows_hbm, ids_hbm, targets_hbm, router_hbm, y_hbm, rank_ref, gate_ref, spot_ref,
    y_ref, rows_ref, ids_ref, targets_ref, router_ref, sems,
):
    loads = start_loads(
        [(targets_hbm, targets_ref), (ids_hbm, ids_ref), (rows_hbm, rows_ref), (router_hbm, router_ref)], sems
    )
    n, width = rows_ref.shape
    for load in loads[:3]:
        load.wait()
    experts = router_ref.shape[1]
    first = iota((n, n), 0)
    second = iota((n, n), 1)
    owner = jnp.broadcast_to((targets_ref[...] // 512).astype(F32), (n, n))
    same = jnp.where((owner.T == owner) & (first < second), 1.0, 0.0)
    place = owner[0:1] * 8.0 + jnp.sum(same, 0, keepdims=True)
    perm = jnp.where(first.astype(F32) == place, 1.0, 0.0)
    spot = (targets_ref[...] % 512).astype(F32)
    spot_ref[...] = jnp.broadcast_to(jnp.sum(perm * spot, 1, keepdims=True), (n, 128))
    perm = perm.astype(BF16)
    rows = dot(perm, rows_ref[...]).astype(BF16)
    ids = dot_t(ids_ref[...].astype(F32).astype(BF16), perm)
    expert = iota((experts, n), 0).astype(F32)
    member = jnp.zeros((experts, n), F32)
    for k in range(ids.shape[0]):
        member = member + jnp.where(expert == ids[k : k + 1, :], 1.0, 0.0)
    before = jnp.where(first < second, 1.0, 0.0).astype(BF16)
    rank = jnp.where(member > 0.5, dot(member.astype(BF16), before), -1.0)
    half = width // 2
    blk = 32
    packed = rank.astype(BF16)
    stores = []
    for i in range(experts // blk):
        spread = jnp.where(iota((blk * 8, experts), 0) // 8 + i * blk == iota((blk * 8, experts), 1), 1.0, 0.0)
        rank_e = dot(spread.astype(BF16), packed)
        slot = (iota(rank_e.shape, 0) % 8).astype(F32)
        main = jnp.where(rank_e == slot, 1.0, 0.0).astype(BF16)
        low = jnp.where((rank_e == slot + 8.0) & (slot < 4.0), 1.0, 0.0).astype(BF16)
        high = jnp.where((rank_e == slot + 4.0) & (slot >= 4.0), 1.0, 0.0).astype(BF16)
        lines = slice(i * blk * 8, (i + 1) * blk * 8)
        y_ref[lines, :width] = dot(main, rows).astype(BF16)
        y_ref[lines, width:] = (dot(low, rows[:, :half]) + dot(high, rows[:, half:])).astype(BF16)
        stores.append(pltpu.make_async_copy(y_ref.at[lines], y_hbm.at[lines], sems.at[4 + i]))
        stores[-1].start()
    rank_ref[...] = rank.T
    member_q = member.T > 0.5
    loads[3].wait()
    logits = dot(rows, router_ref[...])
    highest = jnp.max(jnp.where(member_q, logits, NEG), 1, keepdims=True)
    raised = jnp.where(member_q, jnp.exp(jnp.minimum(logits - highest, 0.0)), 0.0)
    gate_ref[...] = raised / jnp.sum(raised, 1, keepdims=True)
    for store in stores:
        store.wait()


def dispatch(rows, ids, targets, router):
    n, width = rows.shape
    table = jax.ShapeDtypeStruct((n, 128), F32)
    return pl.pallas_call(
        dispatch_kernel,
        in_specs=[pl.BlockSpec(memory_space=pltpu.HBM)] * 4,
        out_specs=[pl.BlockSpec(memory_space=pltpu.HBM)] + [pl.BlockSpec(memory_space=VMEM)] * 3,
        out_shape=[jax.ShapeDtypeStruct((1024, width * 3 // 2), BF16), table, table, table],
        scratch_shapes=[
            VMEM((1024, width * 3 // 2), BF16),
            VMEM((n, width), BF16),
            VMEM((8, n), jnp.int32),
            VMEM((1, n), jnp.int32),
            VMEM(router.shape, BF16),
            pltpu.SemaphoreType.DMA((8,)),
        ],
        compiler_params=pltpu.CompilerParams(vmem_limit_bytes=57 * MIB),
        name="dispatch_rows",
    )(rows, ids.T, targets.reshape(1, n), router)


def expert_kernel(y_ref, wg_ref, wu_ref, wd_ref, o_ref):
    rows = 256
    half_rows = rows // 2
    width = wg_ref.shape[0]
    half = width // 2
    r = iota((half_rows, rows), 0)
    col = iota((half_rows, rows), 1)
    source = r // 4 * 8 + r % 4
    low = jnp.where(col == source, 1.0, 0.0).astype(BF16)
    high = jnp.where(col == source + 4, 1.0, 0.0).astype(BF16)
    rt = iota((rows, half_rows), 0)
    ct = iota((rows, half_rows), 1)
    target = ct // 4 * 8 + ct % 4
    low_t = jnp.where(rt == target, 1.0, 0.0).astype(BF16)
    high_t = jnp.where(rt == target + 4, 1.0, 0.0).astype(BF16)
    for i in range(y_ref.shape[0] // rows):
        lines = slice(i * rows, (i + 1) * rows)
        extra = y_ref[lines, width:]
        inputs = jnp.concatenate(
            [
                y_ref[lines, :width],
                jnp.concatenate([dot(low, extra).astype(BF16), dot(high, extra).astype(BF16)], 1),
            ],
            0,
        )
        gate_part = dot(inputs, wg_ref[...])
        upward = dot(inputs, wu_ref[...])
        hidden = (gate_part / (1.0 + jnp.exp(-gate_part)) * upward).astype(BF16)
        produced = dot(hidden, wd_ref[...]).astype(BF16)
        o_ref[lines, :width] = produced[:rows]
        o_ref[lines, width:] = (dot(low_t, produced[rows:, :half]) + dot(high_t, produced[rows:, half:])).astype(BF16)


def run_expert(y, w_gate, w_up, w_down):
    return pl.pallas_call(
        expert_kernel,
        out_shape=jax.ShapeDtypeStruct(y.shape, BF16),
        compiler_params=pltpu.CompilerParams(vmem_limit_bytes=16 * MIB),
        name="expert_ffn",
    )(y, w_gate, w_up, w_down)


def combine_kernel(r_ref, rank_ref, gate_ref, spot_ref, o_ref):
    n, experts = rank_ref.shape
    rows = r_ref.shape[0]
    width = r_ref.shape[1] * 2 // 3
    spread = jnp.where(iota((experts, rows), 0) == iota((experts, rows), 1) // 8, 1.0, 0.0).astype(BF16)
    gate = gate_ref[...]
    gate_hi = gate.astype(BF16)
    gate_lo = (gate - gate_hi.astype(F32)).astype(BF16)
    rank_e = dot(rank_ref[...].astype(BF16), spread)
    slot = (iota(rank_e.shape, 1) % 8).astype(F32)
    gates = [dot(gate_hi, spread), dot(gate_lo, spread)]

    def chosen(mask):
        return jnp.concatenate([jnp.where(mask, g, 0.0).astype(BF16) for g in gates], 0)

    main = chosen(rank_e == slot)
    extras = [chosen((rank_e == slot + 8.0) & (slot < 4.0)), chosen((rank_e == slot + 4.0) & (slot >= 4.0))]
    spot = spot_ref[...]
    lane = iota(spot.shape, 1)
    big = jnp.floor(spot * (1.0 / 16.0))
    tail = jnp.where(lane == 0, big, jnp.where(lane == 1, spot - 16.0 * big, 0.0))
    tail = tail.reshape(n // 8, 8, 128).astype(BF16)
    parts = o_ref.shape[1]
    w = width // parts
    span = width // 4
    for c in range(4):
        lines = slice(c * span, (c + 1) * span)
        more = width + (c % 2) * span
        merged = dot(main, r_ref[:, lines]) + dot(extras[c // 2], r_ref[:, more : more + span])
        merged = merged[:n] + merged[n:]
        for i in range(span // w):
            o_ref[:, c * (span // w) + i, :, :w] = merged[:, i * w : (i + 1) * w].reshape(n // 8, 8, w).astype(BF16)
    for h in range(parts):
        o_ref[:, h, :, w:] = tail


def combine(r, rank, gate, spot):
    n = rank.shape[0]
    width = r.shape[1] * 2 // 3
    return pl.pallas_call(
        combine_kernel,
        out_shape=jax.ShapeDtypeStruct((n // 8, 8, 8, width // 8 + 128), BF16),
        compiler_params=pltpu.CompilerParams(vmem_limit_bytes=16 * MIB),
        name="combine_rows",
    )(r, rank, gate, spot)


def join_kernel(landed_ref, stream_ref, keep_ref, give_ref):
    core = lax.rem(lax.axis_index("head"), 2)
    tokens, w = stream_ref.shape
    half = tokens // 2
    tail = landed_ref[:, w:].astype(F32)
    spot = tail[:, 0:1] * 16.0 + tail[:, 1:2]
    count = landed_ref.shape[0]
    hit = jnp.where(spot == iota((count, tokens), 1).astype(F32), 1.0, 0.0).astype(BF16)
    added = lax.dot_general(hit, landed_ref[:, :w], (((0,), (0,)), ((), ())), preferred_element_type=F32)
    joined = stream_ref[...].astype(F32) + added
    keep_ref[...] = jnp.where(core == 0, joined[:half], joined[half:]).astype(BF16)
    give_ref[...] = jnp.where(core == 0, joined[half:], joined[:half]).astype(BF16)


def join(landed, stream):
    part = jax.ShapeDtypeStruct((stream.shape[0] // 2, stream.shape[1]), BF16)
    return pl.pallas_call(
        join_kernel,
        out_shape=[part, part],
        compiler_params=pltpu.CompilerParams(vmem_limit_bytes=16 * MIB),
        name="join_rows",
    )(landed, stream)


def turning_tables(tokens, shards):
    frequency = THETA ** (-np.arange(HD // 2, dtype=np.float64) * 2.0 / HD)

    def table(positions):
        angles = np.asarray(positions, np.float64)[:, None] * np.concatenate([frequency, frequency])[None, :]
        return np.stack([np.cos(angles), np.sin(angles)]).astype(np.float32)

    return table(np.arange(tokens)), table(np.arange(shards) * tokens)


def turned(vectors, gains, near, far, shard):
    mean = jnp.mean(vectors * vectors, -1, keepdims=True)
    vectors = vectors * lax.rsqrt(mean + EPSILON) * gains
    far_cos = far[0][pl.ds(shard, 1), :]
    far_sin = far[1][pl.ds(shard, 1), :]
    cos = near[0] * far_cos - near[1] * far_sin
    sin = near[1] * far_cos + near[0] * far_sin
    sign = jnp.where(iota((1, HD), 1) < HD // 2, -1.0, 1.0)
    return vectors * cos + pltpu.roll(vectors, HD // 2, 1) * (sin * sign)


def keys_kernel(x0, x1, x2, x3, gain_ref, kg_ref, wk_hbm, wv_hbm, near_ref, far_ref, kv_ref, norm_ref, wkv_ref, sems):
    ctx = lax.axis_index("ctx")
    head = lax.axis_index("head")
    z = head // 2
    core = lax.rem(head, 2)
    x_refs = (x0, x1, x2, x3)
    columns = pl.ds(pl.multiple_of(z * HD, HD), HD)
    loads = start_loads(
        [(wk_hbm.at[:, columns], wkv_ref.at[:, :HD]), (wv_hbm.at[:, columns], wkv_ref.at[:, HD:])], sems
    )
    _, half, w = x0.shape
    width = 8 * w
    square = jnp.zeros((half, 1), F32)
    for x_ref in x_refs:
        for j in range(2):
            x = x_ref[j].astype(F32)
            square = square + jnp.sum(x * x, 1, keepdims=True)
    scale = lax.rsqrt(square * (1.0 / width) + EPSILON)
    for i, x_ref in enumerate(x_refs):
        for j in range(2):
            block = 2 * lax.rem(z + 4 - i, 4) + (core if j == 0 else 1 - core)
            norm = (x_ref[j].astype(F32) * scale * gain_ref[:, pl.ds(pl.multiple_of(block * w, w), w)]).astype(BF16)
            norm_ref[:, pl.ds(pl.multiple_of(block * w, w), w)] = norm
    for load in loads:
        load.wait()
    both = dot(norm_ref[...], wkv_ref[...])
    shard = jnp.where(core == 0, ctx, far_ref.shape[1] - 1 - ctx)
    near = [jnp.where(core == 0, near_ref[t, :half], near_ref[t, half:]) for t in range(2)]
    far = [far_ref.at[0], far_ref.at[1]]
    kv_ref[:, :HD] = turned(both[:, :HD], kg_ref[pl.ds(z, 1), :], near, far, shard).astype(BF16)
    kv_ref[:, HD:] = both[:, HD:].astype(BF16)


def project_keys(blocks, row_gain, key_gain, w_key, w_value, near, far):
    _, half, w = blocks[0].shape
    return pl.pallas_call(
        keys_kernel,
        in_specs=[pl.BlockSpec(memory_space=VMEM)] * 6
        + [pl.BlockSpec(memory_space=pltpu.HBM)] * 2
        + [pl.BlockSpec(memory_space=VMEM)] * 2,
        out_shape=[jax.ShapeDtypeStruct((half, 2 * HD), BF16), jax.ShapeDtypeStruct((half, 8 * w), BF16)],
        scratch_shapes=[VMEM((w_key.shape[0], 2 * HD), BF16), pltpu.SemaphoreType.DMA((2,))],
        compiler_params=pltpu.CompilerParams(vmem_limit_bytes=16 * MIB),
        name="project_keys",
    )(*blocks, row_gain, key_gain, w_key, w_value, near, far)


def queries_kernel(own_ref, other_ref, wq_ref, qg_ref, near_ref, far_ref, low_ref, high_ref):
    ctx = lax.axis_index("ctx")
    core = lax.rem(lax.axis_index("head"), 2)
    half = own_ref.shape[0]
    factor = math.log2(math.e) / math.sqrt(HD)
    far = [far_ref.at[0], far_ref.at[1]]
    for upper, o_ref in enumerate((low_ref, high_ref)):
        norm = jnp.where(core == upper, own_ref[...], other_ref[...])
        queries = dot(norm, wq_ref[...])
        shard = ctx if upper == 0 else far_ref.shape[1] - 1 - ctx
        near = [near_ref[t, upper * half : (upper + 1) * half] for t in range(2)]
        for h in range(o_ref.shape[0]):
            part = slice(h * HD, (h + 1) * HD)
            o_ref[h] = (turned(queries[:, part], qg_ref[:, part], near, far, shard) * factor).astype(BF16)


def project_queries(own, other, w_query, q_gain, near, far):
    heads = w_query.shape[1] // HD
    part = jax.ShapeDtypeStruct((heads, own.shape[0], HD), BF16)
    return pl.pallas_call(
        queries_kernel,
        out_shape=[part, part],
        compiler_params=pltpu.CompilerParams(vmem_limit_bytes=16 * MIB),
        name="project_queries",
    )(own, other, w_query, q_gain.reshape(1, -1), near, far)


def attend_kernel(low_ref, high_ref, kv_ref, o_ref, value_s):
    ctx = lax.axis_index("ctx")
    core = lax.rem(lax.axis_index("head"), 2)
    shards, shard, _ = kv_ref.shape
    heads, half, _ = low_ref.shape
    group = 4
    subs = 2
    span = group * shard
    rows = heads * half // subs
    value_s[:, :, :HD] = kv_ref[:, :, HD:]
    value_s[:, :, HD:] = jnp.ones((shards, shard, HD), BF16)

    for upper, q_ref in enumerate((low_ref, high_ref)):
        own = ctx if upper == 0 else shards - 1 - ctx
        queries = q_ref[...].reshape(heads * half, HD)
        pieces = [queries[i * rows : (i + 1) * rows] for i in range(subs)]

        def fold(carry, chunk, masked):
            first = jnp.where(core == 0, chunk, shards // group - 1 - chunk) * group
            keys = kv_ref[pl.ds(first, group), :, :HD].reshape(span, HD)
            values = value_s[pl.ds(first, group)].reshape(span, 2 * HD)
            every = [dot_t(piece, keys) for piece in pieces]
            result = []
            for (highest, weighted), scores in zip(carry, every):
                if masked:
                    t = iota((rows, span), 1)
                    place = first + t // shard
                    key_pos = jnp.where(core == 0, place, shards - 1 - place) * (2 * shard) + core * shard + t % shard
                    query_pos = own * (2 * half) + upper * half + iota((rows, span), 0) % half
                    allowed = query_pos >= key_pos
                    scores = jnp.where(allowed, scores, NEG)
                fresh = jnp.maximum(highest, jnp.max(scores, 1, keepdims=True))
                weights = jnp.exp2(scores - fresh)
                if masked:
                    weights = jnp.where(allowed, weights, 0.0)
                weighted = weighted * jnp.exp2(highest - fresh) + dot(weights.astype(BF16), values)
                result.append((fresh, weighted))
            return tuple(result)

        start = tuple((jnp.full((rows, 1), NEG, F32), jnp.zeros((rows, 2 * HD), F32)) for _ in range(subs))
        whole = own // group
        state = lax.fori_loop(0, whole, lambda j, carry: fold(carry, j, False), start)
        state = fold(state, whole, True)
        lane = iota((rows, HD), 1)
        for i, (highest, weighted) in enumerate(state):
            part = slice(i * (heads // subs), (i + 1) * (heads // subs))
            o_ref[part, upper * half : (upper + 1) * half, :HD] = weighted[:, :HD].reshape(heads // subs, half, HD)
            stats = jnp.where(lane < HD // 2, highest, weighted[:, HD:])
            o_ref[part, upper * half : (upper + 1) * half, HD:] = stats.reshape(heads // subs, half, HD)


def attend(low, high, kv):
    heads, half, _ = low.shape
    return pl.pallas_call(
        attend_kernel,
        out_shape=jax.ShapeDtypeStruct((heads, 2 * half, 2 * HD), F32),
        scratch_shapes=[VMEM(kv.shape, BF16)],
        compiler_params=pltpu.CompilerParams(vmem_limit_bytes=28 * MIB),
        name="attend",
    )(low, high, kv)


def project_blocks(attended, core, w_ref, o_ref):
    z = lax.axis_index("head") // 2
    w = o_ref.shape[3]
    for i in range(o_ref.shape[0]):
        for j in range(2):
            block = 2 * lax.rem(z + i, 4) + (core if j == 0 else 1 - core)
            o_ref[i, j] = dot(attended, w_ref[:, pl.ds(pl.multiple_of(block * w, w), w)]).astype(BF16)


def merge_kernel(own_ref, other_ref, w_ref, keep_ref, o_ref):
    core = lax.rem(lax.axis_index("head"), 2)
    half = keep_ref.shape[0]
    given = []
    for h in range(own_ref.shape[0]):
        m0 = own_ref[h, :, HD : HD + 1]
        m1 = other_ref[h, :, HD : HD + 1]
        top = jnp.maximum(m0, m1)
        e0 = jnp.exp2(m0 - top)
        e1 = jnp.exp2(m1 - top)
        total = own_ref[h, :, 2 * HD - 1 :] * e0 + other_ref[h, :, 2 * HD - 1 :] * e1
        share = 1.0 / total
        value = own_ref[h, :, :HD] * (e0 * share) + other_ref[h, :, :HD] * (e1 * share)
        keep_ref[:, h * HD : (h + 1) * HD] = jnp.where(core == 0, value[:half], value[half:]).astype(BF16)
        given.append(jnp.where(core == 0, value[half:], value[:half]).astype(BF16))
    project_blocks(jnp.concatenate(given, 1), 1 - core, w_ref, o_ref)


def own_kernel(attended_ref, w_ref, o_ref):
    project_blocks(attended_ref[...], lax.rem(lax.axis_index("head"), 2), w_ref, o_ref)


def merge_and_project(own, other, w_out):
    heads, tokens, _ = own.shape
    return pl.pallas_call(
        merge_kernel,
        out_shape=[
            jax.ShapeDtypeStruct((tokens // 2, heads * HD), BF16),
            jax.ShapeDtypeStruct((4, 2, tokens // 2, w_out.shape[1] // 8), BF16),
        ],
        compiler_params=pltpu.CompilerParams(vmem_limit_bytes=16 * MIB),
        name="merge_and_project",
    )(own, other, w_out)


def project_own(attended, w_out):
    return pl.pallas_call(
        own_kernel,
        out_shape=jax.ShapeDtypeStruct((4, 2, attended.shape[0], w_out.shape[1] // 8), BF16),
        compiler_params=pltpu.CompilerParams(vmem_limit_bytes=16 * MIB),
        name="project_own",
    )(attended, w_out)


def body(
    branch_rows,
    expert_ids,
    targets,
    router,
    w_gate,
    w_up,
    w_down,
    stream,
    attn_gain,
    q_gain,
    k_gain,
    w_query,
    w_key,
    w_value,
    w_out,
):
    core = lax.axis_index("head") % 2
    experts = router.shape[1]
    tokens, w = stream.shape
    partner = [(i, i ^ 1) for i in range(8)]

    def to_partner(shard):
        return lax.ppermute(shard, "head", partner)

    def along(shard, hops):
        pairs = []
        for c in range(16):
            for h in range(8):
                there = c if h % 2 == 0 else 15 - c
                pairs.append((c * 8 + h, there * 8 + (h + 2 * hops) % 8))
        return lax.ppermute(shard, ("ctx", "head"), pairs)

    def everywhere(blocks):
        return lax.all_to_all(blocks, ("ctx", "head"), split_axis=0, concat_axis=0, tiled=True)

    outgoing, rank, gate, spot = dispatch(branch_rows, expert_ids, targets, router)
    shape = (experts, 8, outgoing.shape[1])
    arrived = everywhere(outgoing.reshape(shape)).reshape(outgoing.shape)
    produced = run_expert(arrived, w_gate[0], w_up[0], w_down[0])
    returned = everywhere(produced.reshape(shape)).reshape(outgoing.shape)
    parcels = combine(returned, rank, gate, spot)
    landed = everywhere(parcels.reshape(experts, 8, parcels.shape[3])).reshape(experts * 8, parcels.shape[3])
    keep, give = join(landed, stream)

    mine = jnp.stack([keep, to_partner(give)])
    blocks = [along(mine, hops) for hops in range(4)]
    near, far = turning_tables(tokens, 16)
    kv, norm = project_keys(blocks, attn_gain.reshape(1, -1), k_gain.reshape(KVH, HD), w_key, w_value, near, far)
    all_kv = lax.all_to_all(
        jnp.broadcast_to(kv[None], (16, *kv.shape)), "ctx", split_axis=0, concat_axis=0, tiled=True
    )
    low, high = project_queries(norm, to_partner(norm), w_query, q_gain, near, far)
    for_partner = attend(to_partner(low), to_partner(high), all_kv)
    from_partner = to_partner(for_partner)
    folded = attend(low, high, all_kv)
    attended, sent = merge_and_project(folded, from_partner, w_out)
    received = to_partner(sent)
    kept = project_own(attended, w_out)
    total = mine.astype(F32)
    for hops in range(4):
        pair = (kept[hops].astype(F32) + received[hops].astype(F32)).astype(BF16)
        total = total + along(pair, hops).astype(F32)
    total = total.astype(BF16)
    other = to_partner(total[1])
    return jnp.where(core == 0, jnp.concatenate([total[0], other], 0), jnp.concatenate([other, total[0]], 0))


def solution(mesh):
    in_specs = (
        P(("ctx", "head"), None),
        P(("ctx", "head"), None),
        P(("ctx", "head")),
        P(),
        P(("ctx", "head"), None, None),
        P(("ctx", "head"), None, None),
        P(("ctx", "head"), None, None),
        P("ctx", "head"),
        P(),
        P("head"),
        P(),
        P(None, "head"),
        P(),
        P(),
        P("head", None),
    )
    out_specs = P("ctx", "head")
    return jax.shard_map(body, mesh=mesh, in_specs=in_specs, out_specs=out_specs, check_vma=False)
```
